256 devices in a mesh: docs: 64 (over x, z, core), terms: 4 (over y).
Axes of the slice: x: 4, y: 4, z: 8, core: 2. Of those that a mesh axis runs over, the one named last changes fastest.
Arguments:
- values: bfloat16 [256, 64, 64, 128], P('docs', 'terms')
- block_ids: int32 [256, 64], P('docs', 'terms'), may hold values from 0 to 2047, as said below
- assignment: int32 [16384, 1], P('docs'), may hold values from 0 to 511
Outputs:
- coefficients: float32 [16384, 512], P('docs', 'terms')
The draws below stay inside these ranges and needn't reach their ends.
Inputs may be any that keep to these rules, and one draw needn't show every extreme that they name: `assignment`: every one of the 512 clusters has at least one document. `block_ids`: in each term slice, the 16 blocks of one tile lie in 16 different ranges of 32 consecutive block numbers, and the tiles of one index of docs place exactly 1 block in each such range.
All inputs are finite; a program needn't handle non-finite values.
Results may differ from the reference program's by a relative error of at most 0.00045.
Values may be sent and summed in bfloat16 or wider, within the bound.
A program may use at most 128 MiB of HBM per device.

```python
import jax
import jax.numpy as jnp
from jax import lax

K = 512
BLOCK = 128
TILE = 64
NNZ = 16
DOCS = 16384
TILES = 256
TILES_DEV = 4
SLOTS = 64
BLK_OWN = 32
BLK_DEV = 2048
N_TERMS = 4


def make_blocks(key):
    base = jax.random.fold_in(key, 11)
    doc_groups = TILES // TILES_DEV
    slices = SLOTS // NNZ
    keys = jax.random.split(base, doc_groups * slices)

    def shuffle(subkey):
        return jax.random.permutation(subkey, doc_groups)
    orders = jax.vmap(shuffle)(keys).reshape(doc_groups, slices, doc_groups)
    pair_index = jnp.arange(TILES_DEV)[:, None] * NNZ + jnp.arange(NNZ)[None, :]
    position = pair_index % doc_groups
    owners = orders[:, :, position]
    owners = jnp.transpose(owners, (0, 2, 1, 3)).reshape(TILES, SLOTS)
    offsets = jax.random.randint(jax.random.fold_in(base, 3), (TILES, SLOTS), 0, BLK_OWN)
    return (owners * BLK_OWN + offsets).astype(jnp.int32)


def draw_block_ids(key, part):
    return make_blocks(key)


def draw_values(key, part):
    keys = jax.random.split(jax.random.fold_in(key, 5), 3)
    shape = (TILES, SLOTS, TILE, BLOCK)
    base = jax.random.normal(keys[0], shape, jnp.float32)
    row_scale = jnp.exp(jax.random.uniform(keys[1], (TILES, 1, TILE, 1), jnp.float32, 0.0, 2.3))
    col_scale = jnp.exp(jax.random.uniform(keys[2], (1, SLOTS, 1, BLOCK), jnp.float32, 0.0, 2.3))
    doc_groups = TILES // TILES_DEV
    owners = (make_blocks(key) // BLK_OWN).astype(jnp.float32)
    owner_rise = 1.0 + 2.0 * owners / max(doc_groups - 1, 1)
    tile_rise = 1.0 + 2.0 * jnp.arange(TILES).astype(jnp.float32) / max(TILES - 1, 1)
    slice_rise = 1.0 + 2.0 * (jnp.arange(SLOTS) // NNZ).astype(jnp.float32) / max(SLOTS // NNZ - 1, 1)
    scaled = 0.02 * base * row_scale * col_scale * owner_rise[:, :, None, None]
    scaled = scaled * tile_rise[:, None, None, None] * slice_rise[None, :, None, None]
    return scaled.astype(jnp.bfloat16)


def choose_distinct(own_key, rows, count, top, lift):
    order = jax.random.permutation(jax.random.fold_in(own_key, 1), count)
    pull = order
    for power in range(3):
        pull = pull * pull // count
    pull = pull * lift // count
    lots = jax.random.randint(jax.random.fold_in(own_key, 2), (rows, count), 0, 4096) + pull
    fixed_rows = jax.random.permutation(jax.random.fold_in(own_key, 3), rows)[jnp.arange(count) % rows]
    lots = jnp.where(jnp.arange(rows)[:, None] == fixed_rows[None, :], 1 << 14, lots)
    priority = lots * count + jnp.arange(count)
    return lax.top_k(priority.astype(jnp.int32), top)[1].astype(jnp.int32)


def setup_inputs(seed: int = 0) -> dict:
    splits = jax.random.split(jax.random.key(seed), 4)
    values = draw_values(jax.random.fold_in(splits[3], 71), 0)
    block_ids = draw_block_ids(jax.random.fold_in(splits[3], 71), 0)
    assignment = choose_distinct(splits[2], DOCS, K, 1, 0)
    return dict(values=values, block_ids=block_ids, assignment=assignment)


EPSILON = 1e-06
RIDGE_WEIGHT = 1.0

def reference(values, block_ids, assignment):
    labels = assignment[:, 0].reshape(TILES, TILE).astype(jnp.int32)

    def slice_sums(index):
        vals = lax.dynamic_slice_in_dim(values, index * NNZ, NNZ, 1)
        blocks = lax.dynamic_slice_in_dim(block_ids, index * NNZ, NNZ, 1)
        segment = (labels[:, None, :] * BLK_DEV + blocks[:, :, None]).astype(jnp.int32)
        flat = vals.astype(jnp.float32).reshape(TILES * NNZ * TILE, BLOCK)
        sums = jax.ops.segment_sum(flat, segment.reshape(-1), num_segments=K * BLK_DEV)
        return (sums.reshape(K, BLK_DEV, BLOCK), vals, blocks)
    slice_index = jnp.arange(N_TERMS, dtype=jnp.int32)

    def add_squares(total, index):
        sums = slice_sums(index)[0]
        return (total + lax.optimization_barrier(jnp.sum(sums * sums, axis=(1, 2))), jnp.zeros((), jnp.float32))
    sq_total, unused = lax.scan(add_squares, jnp.zeros((K,), jnp.float32), slice_index)
    scale = lax.rsqrt(sq_total + EPSILON)

    def add_slice(carry, index):
        gram_matrix, scores = carry
        sums, vals, blocks = slice_sums(index)
        concepts = (sums * scale[:, None, None]).astype(jnp.bfloat16)
        flat = concepts.reshape(K, BLK_DEV * BLOCK).astype(jnp.float32)
        gram_matrix = gram_matrix + jnp.dot(flat.astype(jnp.float32), flat.T.astype(jnp.float32), preferred_element_type=jnp.float32)
        blocks_first = jnp.transpose(concepts, (1, 0, 2))

        def per_tile(inputs):
            tile_values, tile_blocks = inputs
            chosen = blocks_first[tile_blocks].astype(jnp.float32)
            return jnp.einsum('stb,skb->tk', tile_values.astype(jnp.float32), chosen)
        part = lax.map(per_tile, (vals, blocks))
        return ((gram_matrix, scores + part.reshape(DOCS, K)), jnp.zeros((), jnp.float32))
    start = (jnp.zeros((K, K), jnp.float32), jnp.zeros((DOCS, K), jnp.float32))
    totals, unused_two = lax.scan(add_slice, start, slice_index)
    gram_matrix, scores = totals
    identity = jnp.eye(K, dtype=jnp.float32)
    factor = jnp.linalg.cholesky(gram_matrix + RIDGE_WEIGHT * identity)
    inverse = jax.scipy.linalg.cho_solve((factor, True), identity)
    return jnp.dot(scores.astype(jnp.float32), inverse.astype(jnp.float32), precision=lax.Precision.HIGHEST, preferred_element_type=jnp.float32)
```

```python
import functools

import jax
import jax.numpy as jnp
from jax import lax
from jax.experimental import pallas as pl
from jax.experimental.pallas import tpu as pltpu
from jax.sharding import PartitionSpec as P

K = 512
BLK_OWN = 32
NX = 4
NZ = 8
NC = 2
EPSILON = 1e-06
RIDGE_WEIGHT = 1.0
NEWTON_STEPS = 8

F32 = jnp.float32
BF16 = jnp.bfloat16
I32 = jnp.int32
MESH = pl.DeviceIdType.MESH
HI = lax.Precision.HIGHEST
VMEM = pl.BlockSpec(memory_space=pltpu.VMEM)
SMEM = pl.BlockSpec(memory_space=pltpu.SMEM)
ANY = pl.BlockSpec(memory_space=pl.ANY)
DMA = pltpu.SemaphoreType.DMA
VLIM = 60 * 1024 * 1024


def dot_t(a, b, precision=None):
    return lax.dot_general(
        a, b, (((1,), (1,)), ((), ())), precision=precision, preferred_element_type=F32
    )


def coords():
    d = lax.axis_index("docs")
    core = lax.rem(d, NC)
    chip = d // NC
    return chip // NZ, lax.rem(chip, NZ), core, lax.axis_index("terms")


def dev(x, z, core, y):
    return {"docs": (x * NZ + z) * NC + core, "terms": y}


def params(collective_id=None):
    return pltpu.CompilerParams(
        collective_id=collective_id,
        has_side_effects=collective_id is not None,
        vmem_limit_bytes=VLIM,
    )


def order_kernel(ids_ref, v_ref, lab_ref, x_ref, m_ref, c_ref):
    pairs = v_ref.shape[0]
    slots = pairs // lab_ref.shape[0]
    lane = lax.broadcasted_iota(I32, (1, 128), 1)

    def step(p, carry):
        block = ids_ref[p]
        owner = block // BLK_OWN
        tile = p // slots
        code = lax.rem(block, BLK_OWN) * lab_ref.shape[0] + tile
        x_ref[owner] = v_ref[p]
        m_ref[owner] = jnp.where(lane == 64, code, lab_ref[tile])
        return carry

    lax.fori_loop(0, pairs, step, 0)


def order_blocks(values, ids, labels):
    pairs = values.shape[0]

    def kernel(ids_ref, v_ref, lab_ref, x_ref, m_ref):
        order_kernel(ids_ref, v_ref, lab_ref, x_ref, m_ref, None)

    return pl.pallas_call(
        kernel,
        out_shape=(
            jax.ShapeDtypeStruct(values.shape, BF16),
            jax.ShapeDtypeStruct((pairs, 1, 128), I32),
        ),
        in_specs=[SMEM, VMEM, VMEM],
        out_specs=(VMEM, VMEM),
        compiler_params=params(),
        name="order_blocks",
    )(ids, values, labels)


def exchange_kernel(x_ref, m_ref, ox_ref, om_ref, sx, rx, sm, rm, lsem):
    n = x_ref.shape[0]
    me = lax.axis_index("docs")
    barrier = pltpu.get_barrier_semaphore()

    def greet(i, carry):
        peer = lax.rem(me + i, n)
        pl.semaphore_signal(barrier, inc=1, device_id={"docs": peer}, device_id_type=MESH)
        return carry

    lax.fori_loop(1, n, greet, 0)
    own_x = pltpu.make_async_copy(x_ref.at[me], ox_ref.at[me], lsem.at[0])
    own_m = pltpu.make_async_copy(m_ref.at[me], om_ref.at[me], lsem.at[1])
    own_x.start()
    own_m.start()
    pl.semaphore_wait(barrier, n - 1)

    def copies(peer, slot):
        one = pltpu.make_async_remote_copy(
            src_ref=x_ref.at[peer], dst_ref=ox_ref.at[slot],
            send_sem=sx.at[peer], recv_sem=rx.at[slot],
            device_id={"docs": peer}, device_id_type=MESH,
        )
        two = pltpu.make_async_remote_copy(
            src_ref=m_ref.at[peer], dst_ref=om_ref.at[slot],
            send_sem=sm.at[peer], recv_sem=rm.at[slot],
            device_id={"docs": peer}, device_id_type=MESH,
        )
        return one, two

    def send(i, carry):
        one, two = copies(lax.rem(me + i, n), me)
        two.start()
        one.start()
        return carry

    lax.fori_loop(1, n, send, 0)
    own_x.wait()
    own_m.wait()

    def finish(i, carry):
        peer = lax.rem(me + i, n)
        one, two = copies(peer, peer)
        one.wait_recv()
        two.wait_recv()
        one.wait_send()
        two.wait_send()
        return carry

    lax.fori_loop(1, n, finish, 0)


def exchange(x, m):
    n = x.shape[0]
    return pl.pallas_call(
        exchange_kernel,
        out_shape=(jax.ShapeDtypeStruct(x.shape, x.dtype), jax.ShapeDtypeStruct(m.shape, m.dtype)),
        in_specs=[VMEM, VMEM],
        out_specs=(VMEM, VMEM),
        scratch_shapes=[DMA((n,)), DMA((n,)), DMA((n,)), DMA((n,)), DMA((2,))],
        compiler_params=params(0),
        name="exchange_blocks",
    )(x, m)


def sums_kernel(tiles, code_ref, x_ref, m_ref, sums_ref, sq_ref):
    n, rows, _ = x_ref.shape
    sums_ref[...] = jnp.zeros_like(sums_ref)
    cluster = lax.broadcasted_iota(I32, (K, rows), 0)

    def step(a, carry):
        hot = jnp.where(cluster == m_ref[a][:, :rows], 1.0, 0.0).astype(BF16)
        part = jnp.dot(hot, x_ref[a], preferred_element_type=F32)
        block = code_ref[a] // tiles
        sums_ref[block] += part
        return carry

    lax.fori_loop(0, n, step, 0)

    def square(c, total):
        s = sums_ref[c]
        return total + s * s

    total = lax.fori_loop(0, sums_ref.shape[0], square, jnp.zeros((K, 128), F32))
    sq_ref[...] = dot_t(jnp.ones((8, 128), F32), total, HI)[:1]


def own_sums(tiles, code, x, m):
    return pl.pallas_call(
        functools.partial(sums_kernel, tiles),
        out_shape=(
            jax.ShapeDtypeStruct((BLK_OWN, K, 128), F32),
            jax.ShapeDtypeStruct((1, K), F32),
        ),
        in_specs=[SMEM, VMEM, VMEM],
        out_specs=(VMEM, VMEM),
        compiler_params=params(),
        name="own_sums",
    )(code, x, m)


def norm_kernel(ny, sq_ref, scale_ref, slots, zslots, stage, ssem, rsem, zssem, zrsem):
    x, z, core, y = coords()
    group = NX * ny * NC
    me = (x * ny + y) * NC + core
    barrier = pltpu.get_barrier_semaphore()

    def member(g):
        return dev(g // (ny * NC), z, lax.rem(g, NC), lax.rem(g // NC, ny))

    def greet(i, carry):
        pl.semaphore_signal(
            barrier, inc=1, device_id=member(lax.rem(me + i, group)), device_id_type=MESH
        )
        return carry

    lax.fori_loop(1, group, greet, 0)
    for i in range(1, NZ):
        pl.semaphore_signal(
            barrier, inc=1, device_id=dev(x, lax.rem(z + i, NZ), core, y), device_id_type=MESH
        )
    slots[me] = sq_ref[...]
    pl.semaphore_wait(barrier, group - 1 + NZ - 1)

    def copy(peer, slot):
        return pltpu.make_async_remote_copy(
            src_ref=sq_ref, dst_ref=slots.at[slot],
            send_sem=ssem.at[peer], recv_sem=rsem.at[slot],
            device_id=member(peer), device_id_type=MESH,
        )

    def send(i, carry):
        copy(lax.rem(me + i, group), me).start()
        return carry

    lax.fori_loop(1, group, send, 0)

    def finish(i, carry):
        peer = lax.rem(me + i, group)
        done = copy(peer, peer)
        done.wait_recv()
        done.wait_send()
        return carry

    lax.fori_loop(1, group, finish, 0)
    total = jnp.sum(slots[...], axis=0)
    stage[...] = total
    zslots[z] = total

    def zcopy(peer, slot):
        return pltpu.make_async_remote_copy(
            src_ref=stage, dst_ref=zslots.at[slot],
            send_sem=zssem.at[peer], recv_sem=zrsem.at[slot],
            device_id=dev(x, peer, core, y), device_id_type=MESH,
        )

    for i in range(1, NZ):
        zcopy(lax.rem(z + i, NZ), z).start()
    for i in range(1, NZ):
        peer = lax.rem(z + i, NZ)
        done = zcopy(peer, peer)
        done.wait_recv()
        done.wait_send()
    scale_ref[...] = lax.rsqrt(jnp.sum(zslots[...], axis=0) + EPSILON)


def norm_scale(ny, sq):
    group = NX * ny * NC
    return pl.pallas_call(
        functools.partial(norm_kernel, ny),
        out_shape=jax.ShapeDtypeStruct((1, K), F32),
        in_specs=[VMEM],
        out_specs=VMEM,
        scratch_shapes=[
            pltpu.VMEM((group, 1, K), F32),
            pltpu.VMEM((NZ, 1, K), F32),
            pltpu.VMEM((1, K), F32),
            DMA((group,)), DMA((group,)), DMA((NZ,)), DMA((NZ,)),
        ],
        compiler_params=params(1),
        name="norm_scale",
    )(sq)


def axis_peers(ny):
    x, z, core, y = coords()
    peers = {
        "c": [dev(x, z, lax.rem(core + i, NC), y) for i in range(1, NC)],
        "x": [dev(lax.rem(x + i, NX), z, core, y) for i in range(1, NX)],
        "z": [dev(x, lax.rem(z + i, NZ), core, y) for i in range(1, NZ)],
        "y": [dev(x, z, core, lax.rem(y + i, ny)) for i in range(1, ny)],
    }
    return (x, z, core, y), peers


def greet_axes(peers):
    barrier = pltpu.get_barrier_semaphore()
    count = 0
    for axis in "cyxz":
        for peer in peers[axis]:
            pl.semaphore_signal(barrier, inc=1, device_id=peer, device_id_type=MESH)
            count += 1
    return barrier, count


def spread(pos, size, peers, source, target, ssem, rsem):
    def copy(i, send):
        p = lax.rem(pos + i, size)
        return pltpu.make_async_remote_copy(
            src_ref=source(p), dst_ref=target(pos if send else p),
            send_sem=ssem.at[p], recv_sem=rsem.at[pos if send else p],
            device_id=peers[i - 1], device_id_type=MESH,
        )

    for i in range(1, size):
        copy(i, True).start()

    def finish():
        for i in range(1, size):
            done = copy(i, False)
            done.wait_recv()
            done.wait_send()

    return finish


def gram_kernel(ny, sums_ref, scale_ref, out_ref, part, rc, a1, ry, a2, rx, a3, rz,
                cs, cr, ys, yr, xs, xr, zs, zr, xs2, xr2, ys2, yr2, cs2, cr2):
    (x, z, core, y), peers = axis_peers(ny)
    barrier, count = greet_axes(peers)
    blocks = part.shape[0]
    half = blocks // NC
    quarter = half // ny
    rows = part.shape[1]

    scale = jnp.broadcast_to(scale_ref[...], (128, K)).T
    part[...] = jnp.zeros_like(part)
    chunk = 4 if sums_ref.shape[0] % 4 == 0 else 1

    def step(i, carry):
        pieces = [(sums_ref[i * chunk + j] * scale).astype(BF16) for j in range(chunk)]
        c = jnp.concatenate(pieces, axis=1)
        part[...] += dot_t(c, c).reshape(part.shape)
        return carry

    lax.fori_loop(0, sums_ref.shape[0] // chunk, step, 0)
    pl.semaphore_wait(barrier, count)

    finish = spread(core, NC, peers["c"],
                    lambda p: part.at[pl.ds(p * half, half)], lambda p: rc, cs, cr)
    finish()
    a1[...] = part[pl.ds(core * half, half)] + rc[...]
    finish = spread(y, ny, peers["y"],
                    lambda p: a1.at[pl.ds(p * quarter, quarter)], lambda p: ry.at[p], ys, yr)
    ry[y] = a1[pl.ds(y * quarter, quarter)]
    finish()
    total = ry[0]
    for i in range(1, ny):
        total = total + ry[i]
    a2[...] = total
    finish = spread(x, NX, peers["x"], lambda p: a2.at[p], lambda p: rx.at[p], xs, xr)
    rx[x] = a2[x]
    finish()
    total = rx[0]
    for i in range(1, NX):
        total = total + rx[i]
    a3[...] = total
    rz[z] = total
    spread(z, NZ, peers["z"], lambda p: a3, lambda p: rz.at[p], zs, zr)()
    total = rz[0]
    for i in range(1, NZ):
        total = total + rz[i]
    base = core * half + y * quarter
    out_ref[base + x] = total
    spread(x, NX, peers["x"], lambda p: out_ref.at[base + x],
           lambda p: out_ref.at[base + p], xs2, xr2)()
    spread(y, ny, peers["y"], lambda p: out_ref.at[pl.ds(base, quarter)],
           lambda p: out_ref.at[pl.ds(core * half + p * quarter, quarter)], ys2, yr2)()
    spread(core, NC, peers["c"], lambda p: out_ref.at[pl.ds(core * half, half)],
           lambda p: out_ref.at[pl.ds(p * half, half)], cs2, cr2)()


def gram_sum(ny, sums, scale):
    rows = K // (NC * ny * NX)
    blocks = K // rows
    half, quarter = blocks // NC, blocks // (NC * ny)
    sems = []
    for size in (NC, ny, NX, NZ, NX, ny, NC):
        sems += [DMA((size,)), DMA((size,))]
    out = pl.pallas_call(
        functools.partial(gram_kernel, ny),
        out_shape=jax.ShapeDtypeStruct((blocks, rows, K), F32),
        in_specs=[VMEM, VMEM],
        out_specs=VMEM,
        scratch_shapes=[
            pltpu.VMEM((blocks, rows, K), F32),
            pltpu.VMEM((half, rows, K), F32),
            pltpu.VMEM((half, rows, K), F32),
            pltpu.VMEM((ny, quarter, rows, K), F32),
            pltpu.VMEM((quarter, rows, K), F32),
            pltpu.VMEM((NX, rows, K), F32),
            pltpu.VMEM((rows, K), F32),
            pltpu.VMEM((NZ, rows, K), F32),
        ] + sems,
        compiler_params=params(2),
        name="gram_sum",
    )(sums, scale)
    return out.reshape(K, K)


def block_inverse(d):
    n = d.shape[0]
    eye = (lax.broadcasted_iota(I32, (n, n), 0) == lax.broadcasted_iota(I32, (n, n), 1)).astype(F32)
    trace = jnp.sum(d * eye)
    widest = jnp.max(jnp.sum(jnp.abs(d), axis=1, keepdims=True))
    bound = jnp.minimum(trace, widest)
    low = 1.0 / bound
    inv = eye * (1.0 / bound)
    for _ in range(NEWTON_STEPS):
        inv = inv * (2.0 / (1.0 + low))
        left = jnp.dot(d, inv, precision=HI, preferred_element_type=F32)
        inv = 2.0 * inv - jnp.dot(inv, left, precision=HI, preferred_element_type=F32)
        low = 4.0 * low / ((1.0 + low) * (1.0 + low))
    left = jnp.dot(d, inv, precision=HI, preferred_element_type=F32)
    return 2.0 * inv - jnp.dot(inv, left, precision=HI, preferred_element_type=F32)


def inverse_kernel(g_ref, a_ref):
    n = 128
    steps = K // n
    eye = (lax.broadcasted_iota(I32, (K, K), 0) == lax.broadcasted_iota(I32, (K, K), 1)).astype(F32)
    a_ref[...] = g_ref[...] + RIDGE_WEIGHT * eye
    for p in range(steps):
        cut = slice(p * n, (p + 1) * n)
        inv = block_inverse(a_ref[cut, cut])
        row = jnp.dot(inv, a_ref[cut, :], precision=HI, preferred_element_type=F32)
        col = a_ref[:, cut]
        for q in range(steps):
            if q == p:
                continue
            rest = slice(q * n, (q + 1) * n)
            c = col[rest]
            a_ref[rest, :] -= jnp.dot(c, row, precision=HI, preferred_element_type=F32)
            a_ref[rest, cut] = -jnp.dot(c, inv, precision=HI, preferred_element_type=F32)
        a_ref[cut, :] = row
        a_ref[cut, cut] = inv


def ridge_inverse(gram):
    return pl.pallas_call(
        inverse_kernel,
        out_shape=jax.ShapeDtypeStruct((K, K), F32),
        in_specs=[VMEM],
        out_specs=VMEM,
        compiler_params=params(),
        name="ridge_inverse",
    )(gram)


def scores_kernel(tiles, parts, width, *refs):
    first_ref, scale_ref = refs[0], refs[1]
    groups = [refs[2 + 3 * g: 5 + 3 * g] for g in range(len(parts))]
    out_ref, sums_ref, con_ref = refs[2 + 3 * len(parts):]
    rows = groups[0][1].shape[1]
    sums_ref[...] = jnp.zeros_like(sums_ref)
    out_ref[...] = jnp.zeros_like(out_ref)
    cluster = lax.broadcasted_iota(I32, (width, rows), 0) + first_ref[0]

    for (start, count, base), (code_ref, x_ref, m_ref) in zip(parts, groups):
        def add(i, carry):
            spots, sums = [], []
            for u in range(2):
                a = start + 2 * i + u
                hot = jnp.where(cluster == m_ref[a][:, :rows], 1.0, 0.0).astype(BF16)
                sums.append(jnp.dot(hot, x_ref[2 * i + u], preferred_element_type=F32))
                spots.append(code_ref[a] // tiles + base)
            for spot, part in zip(spots, sums):
                sums_ref[spot] += part
            return carry

        lax.fori_loop(0, count // 2, add, 0)

    scale = jnp.broadcast_to(scale_ref[...], (128, width)).T

    def normalise(b, carry):
        con_ref[b] = (sums_ref[b] * scale).astype(BF16)
        return carry

    lax.fori_loop(0, sums_ref.shape[0], normalise, 0)

    for (start, count, base), (code_ref, x_ref, m_ref) in zip(parts, groups):
        def score(i, carry):
            spots, values = [], []
            for u in range(2):
                a = start + 2 * i + u
                code = code_ref[a]
                values.append(dot_t(x_ref[2 * i + u], con_ref[code // tiles + base]))
                spots.append((a, lax.rem(code, tiles)))
            for (a, tile), value in zip(spots, values):
                out_ref[a, tile] += value
            return carry

        lax.fori_loop(0, count // 2, score, 0)


def partial_scores(tiles, first, scale, parts, arrays):
    n = arrays[0][2].shape[0]
    rows = arrays[0][1].shape[1]
    width = scale.shape[1]
    ny = K // width
    flat = [a for group in arrays for a in group]
    return pl.pallas_call(
        functools.partial(scores_kernel, tiles, parts, width),
        out_shape=jax.ShapeDtypeStruct((n, tiles, rows, width), F32),
        in_specs=[SMEM, VMEM] + [SMEM, VMEM, VMEM] * len(parts),
        out_specs=VMEM,
        scratch_shapes=[
            pltpu.VMEM((ny * BLK_OWN, width, 128), F32),
            pltpu.VMEM((ny * BLK_OWN, width, 128), BF16),
        ],
        compiler_params=params(),
        name="partial_scores",
    )(first, scale, *flat)


def scatter_kernel(ny, s_ref, out_ref, rc, acc, rx, a2, rz, lsem,
                   cs, cr, xs, xr, zs, zr, ys, yr):
    (x, z, core, y), peers = axis_peers(ny)
    barrier, count = greet_axes(peers)
    width = rc.shape[-1]
    order = [lax.rem(x + i, NX) for i in range(1, NX)] + [x]
    own = []
    for i, p in enumerate(order):
        copy = pltpu.make_async_copy(s_ref.at[p, :, core], acc.at[p], lsem.at[i])
        copy.start()
        own.append(copy)
    pl.semaphore_wait(barrier, count)
    swap = []
    for i, p in enumerate(order):
        copy = pltpu.make_async_remote_copy(
            src_ref=s_ref.at[p, :, NC - 1 - core], dst_ref=rc.at[p],
            send_sem=cs.at[i], recv_sem=cr.at[i],
            device_id=peers["c"][0], device_id_type=MESH,
        )
        copy.start()
        swap.append(copy)
    sent = []
    for i, p in enumerate(order):
        own[i].wait()
        swap[i].wait_recv()
        acc[p] += rc[p]
        if i < NX - 1:
            copy = pltpu.make_async_remote_copy(
                src_ref=acc.at[p], dst_ref=rx.at[x],
                send_sem=xs.at[i], recv_sem=xr.at[x],
                device_id=peers["x"][i], device_id_type=MESH,
            )
            copy.start()
            sent.append(copy)
    a2[...] = acc[x]
    for i in range(1, NX):
        p = lax.rem(x + i, NX)
        pltpu.make_async_remote_copy(
            src_ref=acc.at[p], dst_ref=rx.at[p],
            send_sem=xs.at[i - 1], recv_sem=xr.at[p],
            device_id=peers["x"][i - 1], device_id_type=MESH,
        ).wait_recv()
        a2[...] += rx[p]
    finish = spread(z, NZ, peers["z"], lambda p: a2.at[p], lambda p: rz.at[p], zs, zr)
    finish()
    rz[z] = a2[z]
    total = rz[0]
    for i in range(1, NZ):
        total = total + rz[i]

    def lanes(p):
        return pl.ds(pl.multiple_of(p * width, width), width)

    out_ref[:, lanes(y)] = total
    spread(y, ny, peers["y"], lambda p: out_ref.at[:, lanes(y)],
           lambda p: out_ref.at[:, lanes(p)], ys, yr)()
    for copy in swap:
        copy.wait_send()
    for copy in sent:
        copy.wait_send()


def scatter_scores(ny, partial):
    n, tiles, rows, width = partial.shape
    docs = tiles * rows
    sems = []
    for size in (NX, NX, NZ, ny):
        sems += [DMA((size,)), DMA((size,))]
    return pl.pallas_call(
        functools.partial(scatter_kernel, ny),
        out_shape=jax.ShapeDtypeStruct((docs, K), F32),
        in_specs=[ANY],
        out_specs=VMEM,
        scratch_shapes=[
            pltpu.VMEM((NX, NZ, docs, width), F32),
            pltpu.VMEM((NX, NZ, docs, width), F32),
            pltpu.VMEM((NX, NZ, docs, width), F32),
            pltpu.VMEM((NZ, docs, width), F32),
            pltpu.VMEM((NZ, docs, width), F32),
            DMA((NX,)),
        ] + sems,
        compiler_params=params(3),
        name="scatter_scores",
    )(partial.reshape(NX, NZ, NC, docs, width))


def shift(array, ny, by):
    return lax.ppermute(array, "terms", [(i, (i + by) % ny) for i in range(ny)])


def body(values, block_ids, assignment):
    tiles, slots, rows, block_width = values.shape
    ny = lax.axis_size("terms")
    pairs = tiles * slots
    width = K // ny
    y = lax.axis_index("terms")
    labels = jnp.pad(
        assignment.reshape(tiles, 1, rows), ((0, 0), (0, 0), (0, 128 - rows)), constant_values=-1
    )
    ordered, meta = order_blocks(
        values.reshape(pairs, rows, block_width), block_ids.reshape(pairs), labels
    )
    own_x, own_m = exchange(ordered, meta)

    def code_of(m):
        return m[:, 0, rows]

    half = pairs // 2
    arrays, parts = [(code_of(own_m), own_x, own_m)], [(0, pairs, 0)]
    up_x, down_x = shift(own_x, ny, 1), shift(own_x, ny, -1)
    up_m = shift(own_m, ny, 1)
    arrays.append((code_of(up_m), up_x, up_m))
    parts.append((0, pairs, BLK_OWN))
    if ny > 2:
        down_m, far_m = shift(own_m, ny, -1), shift(own_m, ny, 2)
        far_a = shift(up_x[:half], ny, 1)
        far_b = shift(down_x[half:], ny, -1)
        arrays.append((code_of(down_m), down_x, down_m))
        parts.append((0, pairs, 3 * BLK_OWN))
        arrays.append((code_of(far_m), far_a, far_m))
        parts.append((0, half, 2 * BLK_OWN))
        arrays.append((code_of(far_m), far_b, far_m))
        parts.append((half, half, 2 * BLK_OWN))

    sums, sq = own_sums(tiles, code_of(own_m), own_x, own_m)
    scale = norm_scale(ny, sq)
    first = (y * width).reshape(1)
    scale_here = lax.dynamic_slice_in_dim(scale, y * width, width, 1)
    partial = partial_scores(tiles, first, scale_here, tuple(parts), arrays)
    gram = gram_sum(ny, sums, scale)
    inverse = ridge_inverse(gram)
    scores = scatter_scores(ny, partial)
    inverse_cols = lax.dynamic_slice_in_dim(inverse, y * width, width, 1)
    return jnp.dot(scores, inverse_cols, precision=HI, preferred_element_type=F32)


def solution(mesh):
    in_specs = (P("docs", "terms", None, None), P("docs", "terms"), P("docs", None))
    out_specs = P("docs", "terms")
    return jax.shard_map(body, mesh=mesh, in_specs=in_specs, out_specs=out_specs, check_vma=False)
```

```python
import functools

import jax
import jax.numpy as jnp
from jax import lax
from jax.experimental import pallas as pl
from jax.experimental.pallas import tpu as pltpu
from jax.sharding import PartitionSpec as P

K = 512
BLK_OWN = 32
NX = 4
NZ = 8
NC = 2
EPSILON = 1e-06
RIDGE_WEIGHT = 1.0
NEWTON_STEPS = 8
UNROLL = 4

F32 = jnp.float32
BF16 = jnp.bfloat16
I32 = jnp.int32
MESH = pl.DeviceIdType.MESH
HI = lax.Precision.HIGHEST
VMEM = pl.BlockSpec(memory_space=pltpu.VMEM)
SMEM = pl.BlockSpec(memory_space=pltpu.SMEM)
ANY = pl.BlockSpec(memory_space=pl.ANY)
DMA = pltpu.SemaphoreType.DMA
VLIM = 60 * 1024 * 1024


def dot_t(a, b, precision=None):
    return lax.dot_general(
        a, b, (((1,), (1,)), ((), ())), precision=precision, preferred_element_type=F32
    )


def coords():
    d = lax.axis_index("docs")
    core = lax.rem(d, NC)
    chip = d // NC
    return chip // NZ, lax.rem(chip, NZ), core, lax.axis_index("terms")


def dev(x, z, core, y):
    return {"docs": (x * NZ + z) * NC + core, "terms": y}


def cost(us):
    return pl.CostEstimate(flops=int(us * 5e8), bytes_accessed=int(us * 2e6), transcendentals=0)


def params(collective_id=None):
    return pltpu.CompilerParams(
        collective_id=collective_id,
        has_side_effects=collective_id is not None,
        vmem_limit_bytes=VLIM,
    )


def order_kernel(ids_ref, v_ref, lab_ref, x_ref, m_ref, c_ref):
    pairs = v_ref.shape[0]
    slots = pairs // lab_ref.shape[0]
    lane = lax.broadcasted_iota(I32, (1, 128), 1)

    def step(p, carry):
        block = ids_ref[p]
        owner = block // BLK_OWN
        tile = p // slots
        code = lax.rem(block, BLK_OWN) * lab_ref.shape[0] + tile
        x_ref[owner] = v_ref[p]
        m_ref[owner] = jnp.where(lane == 64, code, lab_ref[tile])
        return carry

    lax.fori_loop(0, pairs, step, 0)


def order_blocks(values, ids, labels):
    pairs = values.shape[0]

    def kernel(ids_ref, v_ref, lab_ref, x_ref, m_ref):
        order_kernel(ids_ref, v_ref, lab_ref, x_ref, m_ref, None)

    return pl.pallas_call(
        kernel,
        out_shape=(
            jax.ShapeDtypeStruct(values.shape, BF16),
            jax.ShapeDtypeStruct((pairs, 1, 128), I32),
        ),
        in_specs=[SMEM, VMEM, VMEM],
        out_specs=(VMEM, VMEM),
        compiler_params=params(),
        name="order_blocks",
    )(ids, values, labels)


def exchange_kernel(x_ref, m_ref, ox_ref, om_ref, sx, rx, sm, rm, lsem):
    n = x_ref.shape[0]
    me = lax.axis_index("docs")
    barrier = pltpu.get_barrier_semaphore()

    def greet(i, carry):
        peer = lax.rem(me + i, n)
        pl.semaphore_signal(barrier, inc=1, device_id={"docs": peer}, device_id_type=MESH)
        return carry

    lax.fori_loop(1, n, greet, 0)
    own_x = pltpu.make_async_copy(x_ref.at[me], ox_ref.at[me], lsem.at[0])
    own_m = pltpu.make_async_copy(m_ref.at[me], om_ref.at[me], lsem.at[1])
    own_x.start()
    own_m.start()
    pl.semaphore_wait(barrier, n - 1)

    def copies(peer, slot):
        one = pltpu.make_async_remote_copy(
            src_ref=x_ref.at[peer], dst_ref=ox_ref.at[slot],
            send_sem=sx.at[peer], recv_sem=rx.at[slot],
            device_id={"docs": peer}, device_id_type=MESH,
        )
        two = pltpu.make_async_remote_copy(
            src_ref=m_ref.at[peer], dst_ref=om_ref.at[slot],
            send_sem=sm.at[peer], recv_sem=rm.at[slot],
            device_id={"docs": peer}, device_id_type=MESH,
        )
        return one, two

    def send(i, carry):
        one, two = copies(lax.rem(me + i, n), me)
        two.start()
        one.start()
        return carry

    lax.fori_loop(1, n, send, 0)
    own_x.wait()
    own_m.wait()

    def finish(i, carry):
        peer = lax.rem(me + i, n)
        one, two = copies(peer, peer)
        one.wait_recv()
        two.wait_recv()
        one.wait_send()
        two.wait_send()
        return carry

    lax.fori_loop(1, n, finish, 0)


def exchange(x, m):
    n = x.shape[0]
    return pl.pallas_call(
        exchange_kernel,
        out_shape=(jax.ShapeDtypeStruct(x.shape, x.dtype), jax.ShapeDtypeStruct(m.shape, m.dtype)),
        in_specs=[VMEM, VMEM],
        out_specs=(VMEM, VMEM),
        scratch_shapes=[DMA((n,)), DMA((n,)), DMA((n,)), DMA((n,)), DMA((2,))],
        compiler_params=params(0),
        name="exchange_blocks",
    )(x, m)


def sums_kernel(tiles, code_ref, x_ref, m_ref, sums_ref, sq_ref):
    n, rows, _ = x_ref.shape
    sums_ref[...] = jnp.zeros_like(sums_ref)
    cluster = lax.broadcasted_iota(I32, (K, rows), 0)

    def step(i, carry):
        spots, sums = [], []
        for u in range(2):
            a = 2 * i + u
            hot = jnp.where(cluster == m_ref[a][:, :rows], 1.0, 0.0).astype(BF16)
            sums.append(jnp.dot(hot, x_ref[a], preferred_element_type=F32))
            spots.append(code_ref[a] // tiles)
        for spot, part in zip(spots, sums):
            sums_ref[spot] += part
        return carry

    lax.fori_loop(0, n // 2, step, 0)

    def square(c, total):
        s = sums_ref[c]
        return total + s * s

    total = lax.fori_loop(0, sums_ref.shape[0], square, jnp.zeros((K, 128), F32))
    sq_ref[...] = dot_t(jnp.ones((8, 128), F32), total, HI)[:1]


def own_sums(tiles, code, x, m):
    return pl.pallas_call(
        functools.partial(sums_kernel, tiles),
        out_shape=(
            jax.ShapeDtypeStruct((BLK_OWN, K, 128), F32),
            jax.ShapeDtypeStruct((1, K), F32),
        ),
        in_specs=[SMEM, VMEM, VMEM],
        out_specs=(VMEM, VMEM),
        compiler_params=params(),
        cost_estimate=cost(17),
        name="own_sums",
    )(code, x, m)


def norm_kernel(ny, sq_ref, scale_ref, slots, zslots, stage, ssem, rsem, zssem, zrsem):
    x, z, core, y = coords()
    group = NX * ny * NC
    me = (x * ny + y) * NC + core
    barrier = pltpu.get_barrier_semaphore()

    def member(g):
        return dev(g // (ny * NC), z, lax.rem(g, NC), lax.rem(g // NC, ny))

    def greet(i, carry):
        pl.semaphore_signal(
            barrier, inc=1, device_id=member(lax.rem(me + i, group)), device_id_type=MESH
        )
        return carry

    lax.fori_loop(1, group, greet, 0)
    for i in range(1, NZ):
        pl.semaphore_signal(
            barrier, inc=1, device_id=dev(x, lax.rem(z + i, NZ), core, y), device_id_type=MESH
        )
    slots[me] = sq_ref[...]
    pl.semaphore_wait(barrier, group - 1 + NZ - 1)

    def copy(peer, slot):
        return pltpu.make_async_remote_copy(
            src_ref=sq_ref, dst_ref=slots.at[slot],
            send_sem=ssem.at[peer], recv_sem=rsem.at[slot],
            device_id=member(peer), device_id_type=MESH,
        )

    def send(i, carry):
        copy(lax.rem(me + i, group), me).start()
        return carry

    lax.fori_loop(1, group, send, 0)

    def finish(i, carry):
        peer = lax.rem(me + i, group)
        done = copy(peer, peer)
        done.wait_recv()
        done.wait_send()
        return carry

    lax.fori_loop(1, group, finish, 0)
    total = jnp.sum(slots[...], axis=0)
    stage[...] = total
    zslots[z] = total

    def zcopy(peer, slot):
        return pltpu.make_async_remote_copy(
            src_ref=stage, dst_ref=zslots.at[slot],
            send_sem=zssem.at[peer], recv_sem=zrsem.at[slot],
            device_id=dev(x, peer, core, y), device_id_type=MESH,
        )

    for i in range(1, NZ):
        zcopy(lax.rem(z + i, NZ), z).start()
    for i in range(1, NZ):
        peer = lax.rem(z + i, NZ)
        done = zcopy(peer, peer)
        done.wait_recv()
        done.wait_send()
    scale_ref[...] = lax.rsqrt(jnp.sum(zslots[...], axis=0) + EPSILON)


def norm_scale(ny, sq):
    group = NX * ny * NC
    return pl.pallas_call(
        functools.partial(norm_kernel, ny),
        out_shape=jax.ShapeDtypeStruct((1, K), F32),
        in_specs=[VMEM],
        out_specs=VMEM,
        scratch_shapes=[
            pltpu.VMEM((group, 1, K), F32),
            pltpu.VMEM((NZ, 1, K), F32),
            pltpu.VMEM((1, K), F32),
            DMA((group,)), DMA((group,)), DMA((NZ,)), DMA((NZ,)),
        ],
        compiler_params=params(1),
        cost_estimate=cost(17),
        name="norm_scale",
    )(sq)


def axis_peers(ny):
    x, z, core, y = coords()
    peers = {
        "c": [dev(x, z, lax.rem(core + i, NC), y) for i in range(1, NC)],
        "x": [dev(lax.rem(x + i, NX), z, core, y) for i in range(1, NX)],
        "z": [dev(x, lax.rem(z + i, NZ), core, y) for i in range(1, NZ)],
        "y": [dev(x, z, core, lax.rem(y + i, ny)) for i in range(1, ny)],
    }
    return (x, z, core, y), peers


def greet_axes(peers):
    barrier = pltpu.get_barrier_semaphore()
    count = 0
    for axis in "cyxz":
        for peer in peers[axis]:
            pl.semaphore_signal(barrier, inc=1, device_id=peer, device_id_type=MESH)
            count += 1
    return barrier, count


def spread(pos, size, peers, source, target, ssem, rsem):
    def copy(i, send):
        p = lax.rem(pos + i, size)
        return pltpu.make_async_remote_copy(
            src_ref=source(p), dst_ref=target(pos if send else p),
            send_sem=ssem.at[p], recv_sem=rsem.at[pos if send else p],
            device_id=peers[i - 1], device_id_type=MESH,
        )

    for i in range(1, size):
        copy(i, True).start()

    def finish():
        for i in range(1, size):
            done = copy(i, False)
            done.wait_recv()
            done.wait_send()

    return finish


def block_inverse(d):
    n = d.shape[0]
    eye = (lax.broadcasted_iota(I32, (n, n), 0) == lax.broadcasted_iota(I32, (n, n), 1)).astype(F32)
    trace = jnp.sum(d * eye)
    widest = jnp.max(jnp.sum(jnp.abs(d), axis=1, keepdims=True))
    bound = jnp.minimum(trace, widest)
    low = 1.0 / bound
    inv = eye * (1.0 / bound)
    for _ in range(NEWTON_STEPS):
        inv = inv * (2.0 / (1.0 + low))
        left = jnp.dot(d, inv, precision=HI, preferred_element_type=F32)
        inv = 2.0 * inv - jnp.dot(inv, left, precision=HI, preferred_element_type=F32)
        low = 4.0 * low / ((1.0 + low) * (1.0 + low))
    left = jnp.dot(d, inv, precision=HI, preferred_element_type=F32)
    return 2.0 * inv - jnp.dot(inv, left, precision=HI, preferred_element_type=F32)


def scores_kernel(tiles, parts, width, *refs):
    first_ref, scale_ref = refs[0], refs[1]
    groups = [refs[2 + 3 * g: 5 + 3 * g] for g in range(len(parts))]
    out_ref, sums_ref, con_ref = refs[2 + 3 * len(parts):]
    rows = groups[0][1].shape[1]
    sums_ref[...] = jnp.zeros_like(sums_ref)
    out_ref[...] = jnp.zeros_like(out_ref)
    cluster = lax.broadcasted_iota(I32, (width, rows), 0) + first_ref[0]

    for (start, count, base), (code_ref, x_ref, m_ref) in zip(parts, groups):
        def add(i, carry):
            spots, sums = [], []
            for u in range(UNROLL):
                a = start + UNROLL * i + u
                hot = jnp.where(cluster == m_ref[a][:, :rows], 1.0, 0.0).astype(BF16)
                sums.append(jnp.dot(hot, x_ref[UNROLL * i + u], preferred_element_type=F32))
                spots.append(code_ref[a] // tiles + base)
            for spot, part in zip(spots, sums):
                sums_ref[spot] += part
            return carry

        lax.fori_loop(0, count // UNROLL, add, 0)

    scale = jnp.broadcast_to(scale_ref[...], (128, width)).T

    def normalise(b, carry):
        con_ref[b] = (sums_ref[b] * scale).astype(BF16)
        return carry

    lax.fori_loop(0, sums_ref.shape[0], normalise, 0)

    for (start, count, base), (code_ref, x_ref, m_ref) in zip(parts, groups):
        def score(i, carry):
            spots, values = [], []
            for u in range(UNROLL):
                a = start + UNROLL * i + u
                code = code_ref[a]
                values.append(dot_t(x_ref[UNROLL * i + u], con_ref[code // tiles + base]))
                spots.append((a, lax.rem(code, tiles)))
            for (a, tile), value in zip(spots, values):
                out_ref[a, tile] += value
            return carry

        lax.fori_loop(0, count // UNROLL, score, 0)


def partial_scores(tiles, first, scale, parts, arrays):
    n = arrays[0][2].shape[0]
    rows = arrays[0][1].shape[1]
    width = scale.shape[1]
    ny = K // width
    flat = [a for group in arrays for a in group]
    return pl.pallas_call(
        functools.partial(scores_kernel, tiles, parts, width),
        out_shape=jax.ShapeDtypeStruct((n, tiles, rows, width), F32),
        in_specs=[SMEM, VMEM] + [SMEM, VMEM, VMEM] * len(parts),
        out_specs=VMEM,
        scratch_shapes=[
            pltpu.VMEM((ny * BLK_OWN, width, 128), F32),
            pltpu.VMEM((ny * BLK_OWN, width, 128), BF16),
        ],
        compiler_params=params(),
        cost_estimate=cost(45),
        name="partial_scores",
    )(first, scale, *flat)


def gram_part(sums_ref, scale_ref, part):
    scale = jnp.broadcast_to(scale_ref[...], (128, K)).T
    part[...] = jnp.zeros_like(part)
    chunk = 4

    def step(i, carry):
        pieces = [(sums_ref[i * chunk + j] * scale).astype(BF16) for j in range(chunk)]
        c = jnp.concatenate(pieces, axis=1)
        part[...] += dot_t(c, c).reshape(part.shape)
        return carry

    lax.fori_loop(0, sums_ref.shape[0] // chunk, step, 0)


def inverse_panel(a_ref, p):
    n = 128
    cut = slice(p * n, (p + 1) * n)
    inv = block_inverse(a_ref[cut, cut])
    row = jnp.dot(inv, a_ref[cut, :], precision=HI, preferred_element_type=F32)
    col = a_ref[:, cut]
    for q in range(K // n):
        if q == p:
            continue
        rest = slice(q * n, (q + 1) * n)
        c = col[rest]
        a_ref[rest, :] -= jnp.dot(c, row, precision=HI, preferred_element_type=F32)
        a_ref[rest, cut] = -jnp.dot(c, inv, precision=HI, preferred_element_type=F32)
    a_ref[cut, :] = row
    a_ref[cut, cut] = inv


def reduce_kernel(ny, s_ref, sums_ref, scale_ref, scores_ref, a_ref,
                  rc, acc, rx, rz, lsem,
                  part, gc, a1, gy, a2, gx, a3, gz, gram,
                  cs, cr, xs, xr, zs, zr, ys, yr,
                  gcs, gcr, gys, gyr, gxs, gxr, gzs, gzr,
                  gxs2, gxr2, gys2, gyr2, gcs2, gcr2):
    (x, z, core, y), peers = axis_peers(ny)
    barrier, count = greet_axes(peers)
    width = rc.shape[-1]
    order = [lax.rem(x + i, NX) for i in (NX - 1, 1, 2, 0)]
    own = []
    for i, p in enumerate(order):
        copy = pltpu.make_async_copy(s_ref.at[p, :, core], acc.at[p], lsem.at[i])
        copy.start()
        own.append(copy)
    pl.semaphore_wait(barrier, count)
    swap = []
    for i, p in enumerate(order):
        copy = pltpu.make_async_remote_copy(
            src_ref=s_ref.at[p, :, NC - 1 - core], dst_ref=rc.at[p],
            send_sem=cs.at[i], recv_sem=cr.at[i],
            device_id=peers["c"][0], device_id_type=MESH,
        )
        copy.start()
        swap.append(copy)

    def pair(i):
        own[i].wait()
        swap[i].wait_recv()
        acc[order[i]] += rc[order[i]]

    cut = NZ // 2
    upper, lower = peers["x"][0], peers["x"][NX - 2]

    def hop(s, down):
        sent = lax.rem(x + (s + 1 if down else 2 * NX - s - 1), NX)
        part_z = pl.ds(cut if down else 0, cut)
        return pltpu.make_async_remote_copy(
            src_ref=acc.at[sent, part_z], dst_ref=rx.at[s, part_z],
            send_sem=xs.at[2 * s + down], recv_sem=xr.at[2 * s + down],
            device_id=lower if down else upper, device_id_type=MESH,
        )

    def land(s, down):
        hop(s, down).wait_recv()
        got = lax.rem(x + (s + 2 if down else 2 * NX - s - 2), NX)
        part_z = pl.ds(cut if down else 0, cut)
        acc[got, part_z] += rx[s, part_z]

    blocks = part.shape[0]
    half = blocks // NC
    quarter = half // ny

    gram_part(sums_ref, scale_ref, part)
    finish = spread(core, NC, peers["c"],
                    lambda p: part.at[pl.ds(p * half, half)], lambda p: gc, gcs, gcr)
    pair(0)
    hop(0, 0).start()
    pair(1)
    hop(0, 1).start()
    finish()
    a1[...] = part[pl.ds(core * half, half)] + gc[...]
    finish = spread(y, ny, peers["y"],
                    lambda p: a1.at[pl.ds(p * quarter, quarter)], lambda p: gy.at[p], gys, gyr)
    pair(2)
    pair(3)
    gy[y] = a1[pl.ds(y * quarter, quarter)]
    finish()
    total = gy[0]
    for i in range(1, ny):
        total = total + gy[i]
    a2[...] = total
    finish = spread(x, NX, peers["x"], lambda p: a2.at[p], lambda p: gx.at[p], gxs, gxr)
    gx[x] = a2[x]
    for down in range(2):
        land(0, down)
        hop(1, down).start()
    finish()
    total = gx[0]
    for i in range(1, NX):
        total = total + gx[i]
    a3[...] = total
    gz[z] = total
    spread(z, NZ, peers["z"], lambda p: a3, lambda p: gz.at[p], gzs, gzr)()
    total = gz[0]
    for i in range(1, NZ):
        total = total + gz[i]
    base = core * half + y * quarter
    gram[base + x] = total
    finish = spread(x, NX, peers["x"], lambda p: gram.at[base + x],
                    lambda p: gram.at[base + p], gxs2, gxr2)
    for down in range(2):
        land(1, down)
        hop(2, down).start()
    finish()
    spread(y, ny, peers["y"], lambda p: gram.at[pl.ds(base, quarter)],
           lambda p: gram.at[pl.ds(core * half + p * quarter, quarter)], gys2, gyr2)()
    spread(core, NC, peers["c"], lambda p: gram.at[pl.ds(core * half, half)],
           lambda p: gram.at[pl.ds(p * half, half)], gcs2, gcr2)()

    eye = (lax.broadcasted_iota(I32, (K, K), 0) == lax.broadcasted_iota(I32, (K, K), 1)).astype(F32)
    a_ref[...] = gram[...].reshape(K, K) + RIDGE_WEIGHT * eye
    for down in range(2):
        land(2, down)
    finish = spread(z, NZ, peers["z"], lambda p: acc.at[x, p], lambda p: rz.at[p], zs, zr)
    for p in range(K // 128):
        inverse_panel(a_ref, p)
    rz[z] = acc[x, z]
    finish()
    total = rz[0]
    for i in range(1, NZ):
        total = total + rz[i]

    def lanes(p):
        return pl.ds(pl.multiple_of(p * width, width), width)

    scores_ref[:, lanes(y)] = total
    spread(y, ny, peers["y"], lambda p: scores_ref.at[:, lanes(y)],
           lambda p: scores_ref.at[:, lanes(p)], ys, yr)()
    for copy in swap:
        copy.wait_send()
    for s in range(NX - 1):
        for down in range(2):
            hop(s, down).wait_send()


def reduce_scores(ny, partial, sums, scale):
    n, tiles, rows, width = partial.shape
    docs = tiles * rows
    part_rows = K // (NC * ny * NX)
    blocks = K // part_rows
    half, quarter = blocks // NC, blocks // (NC * ny)
    sems = []
    for size in (NX, 2 * (NX - 1), NZ, ny, NC, ny, NX, NZ, NX, ny, NC):
        sems += [DMA((size,)), DMA((size,))]
    return pl.pallas_call(
        functools.partial(reduce_kernel, ny),
        out_shape=(jax.ShapeDtypeStruct((docs, K), F32), jax.ShapeDtypeStruct((K, K), F32)),
        in_specs=[ANY, VMEM, VMEM],
        out_specs=(VMEM, VMEM),
        scratch_shapes=[
            pltpu.VMEM((NX, NZ, docs, width), F32),
            pltpu.VMEM((NX, NZ, docs, width), F32),
            pltpu.VMEM((NX - 1, NZ, docs, width), F32),
            pltpu.VMEM((NZ, docs, width), F32),
            DMA((NX,)),
            pltpu.VMEM((blocks, part_rows, K), F32),
            pltpu.VMEM((half, part_rows, K), F32),
            pltpu.VMEM((half, part_rows, K), F32),
            pltpu.VMEM((ny, quarter, part_rows, K), F32),
            pltpu.VMEM((quarter, part_rows, K), F32),
            pltpu.VMEM((NX, part_rows, K), F32),
            pltpu.VMEM((part_rows, K), F32),
            pltpu.VMEM((NZ, part_rows, K), F32),
            pltpu.VMEM((blocks, part_rows, K), F32),
        ] + sems,
        compiler_params=params(2),
        name="reduce_scores",
    )(partial.reshape(NX, NZ, NC, docs, width), sums, scale)


def shift(array, ny, by):
    return lax.ppermute(array, "terms", [(i, (i + by) % ny) for i in range(ny)])


def body(values, block_ids, assignment):
    tiles, slots, rows, block_width = values.shape
    ny = lax.axis_size("terms")
    pairs = tiles * slots
    width = K // ny
    y = lax.axis_index("terms")
    labels = jnp.pad(
        assignment.reshape(tiles, 1, rows), ((0, 0), (0, 0), (0, 128 - rows)), constant_values=-1
    )
    ordered, meta = order_blocks(
        values.reshape(pairs, rows, block_width), block_ids.reshape(pairs), labels
    )
    own_x, own_m = exchange(ordered, meta)

    def code_of(m):
        return m[:, 0, rows]

    half = pairs // 2
    arrays, parts = [(code_of(own_m), own_x, own_m)], [(0, pairs, 0)]
    up_x, down_x = shift(own_x, ny, 1), shift(own_x, ny, -1)
    up_m = shift(own_m, ny, 1)
    arrays.append((code_of(up_m), up_x, up_m))
    parts.append((0, pairs, BLK_OWN))
    if ny > 2:
        down_m, far_m = shift(own_m, ny, -1), shift(own_m, ny, 2)
        far_a = shift(up_x[:half], ny, 1)
        far_b = shift(down_x[half:], ny, -1)
        arrays.append((code_of(down_m), down_x, down_m))
        parts.append((0, pairs, 3 * BLK_OWN))
        arrays.append((code_of(far_m), far_a, far_m))
        parts.append((0, half, 2 * BLK_OWN))
        arrays.append((code_of(far_m), far_b, far_m))
        parts.append((half, half, 2 * BLK_OWN))

    sums, sq = own_sums(tiles, code_of(own_m), own_x, own_m)
    scale = norm_scale(ny, sq)
    first = (y * width).reshape(1)
    scale_here = lax.dynamic_slice_in_dim(scale, y * width, width, 1)
    partial = partial_scores(tiles, first, scale_here, tuple(parts), arrays)
    scores, inverse = reduce_scores(ny, partial, sums, scale)
    inverse_cols = lax.dynamic_slice_in_dim(inverse, y * width, width, 1)
    return jnp.dot(scores, inverse_cols, precision=HI, preferred_element_type=F32)


def solution(mesh):
    in_specs = (P("docs", "terms", None, None), P("docs", "terms"), P("docs", None))
    out_specs = P("docs", "terms")
    return jax.shard_map(body, mesh=mesh, in_specs=in_specs, out_specs=out_specs, check_vma=False)
```

```python
import functools

import jax
import jax.numpy as jnp
from jax import lax
from jax.experimental import pallas as pl
from jax.experimental.pallas import tpu as pltpu
from jax.sharding import PartitionSpec as P

K = 512
BLK_OWN = 32
NX = 4
NZ = 8
NC = 2
EPSILON = 1e-06
RIDGE_WEIGHT = 1.0
NEWTON_STEPS = 8
UNROLL = 8

F32 = jnp.float32
BF16 = jnp.bfloat16
I32 = jnp.int32
MESH = pl.DeviceIdType.MESH
HI = lax.Precision.HIGHEST
VMEM = pl.BlockSpec(memory_space=pltpu.VMEM)
SMEM = pl.BlockSpec(memory_space=pltpu.SMEM)
ANY = pl.BlockSpec(memory_space=pl.ANY)
DMA = pltpu.SemaphoreType.DMA
VLIM = 60 * 1024 * 1024


def dot_t(a, b, precision=None):
    return lax.dot_general(
        a, b, (((1,), (1,)), ((), ())), precision=precision, preferred_element_type=F32
    )


def coords():
    d = lax.axis_index("docs")
    core = lax.rem(d, NC)
    chip = d // NC
    return chip // NZ, lax.rem(chip, NZ), core, lax.axis_index("terms")


def dev(x, z, core, y):
    return {"docs": (x * NZ + z) * NC + core, "terms": y}


def cost(us):
    return pl.CostEstimate(flops=int(us * 5e8), bytes_accessed=int(us * 2e6), transcendentals=0)


def params(collective_id=None):
    return pltpu.CompilerParams(
        collective_id=collective_id,
        has_side_effects=collective_id is not None,
        vmem_limit_bytes=VLIM,
    )


def order_kernel(ids_ref, v_ref, lab_ref, x_ref, m_ref, c_ref):
    pairs = v_ref.shape[0]
    slots = pairs // lab_ref.shape[0]
    lane = lax.broadcasted_iota(I32, (1, 128), 1)

    def step(p, carry):
        block = ids_ref[p // slots, lax.rem(p, slots)]
        owner = block // BLK_OWN
        tile = p // slots
        code = lax.rem(block, BLK_OWN) * lab_ref.shape[0] + tile
        x_ref[owner] = v_ref[p]
        m_ref[owner] = jnp.where(lane == 64, code, lab_ref[tile])
        return carry

    lax.fori_loop(0, pairs, step, 0)


def order_blocks(values, ids, labels):
    pairs = values.shape[0]

    def kernel(ids_ref, v_ref, lab_ref, x_ref, m_ref):
        order_kernel(ids_ref, v_ref, lab_ref, x_ref, m_ref, None)

    return pl.pallas_call(
        kernel,
        out_shape=(
            jax.ShapeDtypeStruct(values.shape, BF16),
            jax.ShapeDtypeStruct((pairs, 1, 128), I32),
        ),
        in_specs=[SMEM, VMEM, VMEM],
        out_specs=(VMEM, VMEM),
        compiler_params=params(),
        name="order_blocks",
    )(ids, values, labels)


def exchange_kernel(x_ref, m_ref, ox_ref, om_ref, sx, rx, sm, rm, lsem):
    n = x_ref.shape[0]
    me = lax.axis_index("docs")
    barrier = pltpu.get_barrier_semaphore()

    def greet(i, carry):
        peer = lax.rem(me + i, n)
        pl.semaphore_signal(barrier, inc=1, device_id={"docs": peer}, device_id_type=MESH)
        return carry

    lax.fori_loop(1, n, greet, 0)
    own_x = pltpu.make_async_copy(x_ref.at[me], ox_ref.at[me], lsem.at[0])
    own_m = pltpu.make_async_copy(m_ref.at[me], om_ref.at[me], lsem.at[1])
    own_x.start()
    own_m.start()
    pl.semaphore_wait(barrier, n - 1)

    def copies(peer, slot):
        one = pltpu.make_async_remote_copy(
            src_ref=x_ref.at[peer], dst_ref=ox_ref.at[slot],
            send_sem=sx.at[peer], recv_sem=rx.at[slot],
            device_id={"docs": peer}, device_id_type=MESH,
        )
        two = pltpu.make_async_remote_copy(
            src_ref=m_ref.at[peer], dst_ref=om_ref.at[slot],
            send_sem=sm.at[peer], recv_sem=rm.at[slot],
            device_id={"docs": peer}, device_id_type=MESH,
        )
        return one, two

    def send(i, carry):
        one, two = copies(lax.rem(me + i, n), me)
        two.start()
        one.start()
        return carry

    lax.fori_loop(1, n, send, 0)
    own_x.wait()
    own_m.wait()

    def finish(i, carry):
        peer = lax.rem(me + i, n)
        one, two = copies(peer, peer)
        one.wait_recv()
        two.wait_recv()
        one.wait_send()
        two.wait_send()
        return carry

    lax.fori_loop(1, n, finish, 0)


def exchange(x, m):
    n = x.shape[0]
    return pl.pallas_call(
        exchange_kernel,
        out_shape=(jax.ShapeDtypeStruct(x.shape, x.dtype), jax.ShapeDtypeStruct(m.shape, m.dtype)),
        in_specs=[VMEM, VMEM],
        out_specs=(VMEM, VMEM),
        scratch_shapes=[DMA((n,)), DMA((n,)), DMA((n,)), DMA((n,)), DMA((2,))],
        compiler_params=params(0),
        name="exchange_blocks",
    )(x, m)


def sums_kernel(tiles, code_ref, x_ref, m_ref, sums_ref, sq_ref):
    n, rows, _ = x_ref.shape
    sums_ref[...] = jnp.zeros_like(sums_ref)
    cluster = lax.broadcasted_iota(I32, (K, rows), 0)

    def step(i, carry):
        spots, sums = [], []
        for u in range(4):
            a = 4 * i + u
            hot = jnp.where(cluster == m_ref[a][:, :rows], 1.0, 0.0).astype(BF16)
            sums.append(jnp.dot(hot, x_ref[a], preferred_element_type=F32))
            spots.append(code_ref[a, 0, rows] // tiles)
        for spot, part in zip(spots, sums):
            sums_ref[spot] += part
        return carry

    lax.fori_loop(0, n // 4, step, 0)

    def square(c, total):
        s = sums_ref[c]
        return total + s * s

    total = lax.fori_loop(0, sums_ref.shape[0], square, jnp.zeros((K, 128), F32))
    sq_ref[...] = dot_t(jnp.ones((8, 128), F32), total, HI)[:1]


def own_sums(tiles, code, x, m):
    return pl.pallas_call(
        functools.partial(sums_kernel, tiles),
        out_shape=(
            jax.ShapeDtypeStruct((BLK_OWN, K, 128), F32),
            jax.ShapeDtypeStruct((1, K), F32),
        ),
        in_specs=[SMEM, VMEM, VMEM],
        out_specs=(VMEM, VMEM),
        compiler_params=params(),
        cost_estimate=cost(17),
        name="own_sums",
    )(code, x, m)


def norm_kernel(ny, sq_ref, scale_ref, slots, zslots, stage, ssem, rsem, zssem, zrsem):
    x, z, core, y = coords()
    group = NX * ny * NC
    me = (x * ny + y) * NC + core
    barrier = pltpu.get_barrier_semaphore()

    def member(g):
        return dev(g // (ny * NC), z, lax.rem(g, NC), lax.rem(g // NC, ny))

    def greet(i, carry):
        pl.semaphore_signal(
            barrier, inc=1, device_id=member(lax.rem(me + i, group)), device_id_type=MESH
        )
        return carry

    lax.fori_loop(1, group, greet, 0)
    for i in range(1, NZ):
        pl.semaphore_signal(
            barrier, inc=1, device_id=dev(x, lax.rem(z + i, NZ), core, y), device_id_type=MESH
        )
    slots[me] = sq_ref[...]
    pl.semaphore_wait(barrier, group - 1 + NZ - 1)

    def copy(peer, slot):
        return pltpu.make_async_remote_copy(
            src_ref=sq_ref, dst_ref=slots.at[slot],
            send_sem=ssem.at[peer], recv_sem=rsem.at[slot],
            device_id=member(peer), device_id_type=MESH,
        )

    def send(i, carry):
        copy(lax.rem(me + i, group), me).start()
        return carry

    lax.fori_loop(1, group, send, 0)

    def finish(i, carry):
        peer = lax.rem(me + i, group)
        done = copy(peer, peer)
        done.wait_recv()
        done.wait_send()
        return carry

    lax.fori_loop(1, group, finish, 0)
    total = jnp.sum(slots[...], axis=0)
    stage[...] = total
    zslots[z] = total

    def zcopy(peer, slot):
        return pltpu.make_async_remote_copy(
            src_ref=stage, dst_ref=zslots.at[slot],
            send_sem=zssem.at[peer], recv_sem=zrsem.at[slot],
            device_id=dev(x, peer, core, y), device_id_type=MESH,
        )

    for i in range(1, NZ):
        zcopy(lax.rem(z + i, NZ), z).start()
    for i in range(1, NZ):
        peer = lax.rem(z + i, NZ)
        done = zcopy(peer, peer)
        done.wait_recv()
        done.wait_send()
    scale_ref[...] = lax.rsqrt(jnp.sum(zslots[...], axis=0) + EPSILON)


def norm_scale(ny, sq):
    group = NX * ny * NC
    return pl.pallas_call(
        functools.partial(norm_kernel, ny),
        out_shape=jax.ShapeDtypeStruct((1, K), F32),
        in_specs=[VMEM],
        out_specs=VMEM,
        scratch_shapes=[
            pltpu.VMEM((group, 1, K), F32),
            pltpu.VMEM((NZ, 1, K), F32),
            pltpu.VMEM((1, K), F32),
            DMA((group,)), DMA((group,)), DMA((NZ,)), DMA((NZ,)),
        ],
        compiler_params=params(1),
        cost_estimate=cost(17),
        name="norm_scale",
    )(sq)


def axis_peers(ny):
    x, z, core, y = coords()
    peers = {
        "c": [dev(x, z, lax.rem(core + i, NC), y) for i in range(1, NC)],
        "x": [dev(lax.rem(x + i, NX), z, core, y) for i in range(1, NX)],
        "z": [dev(x, lax.rem(z + i, NZ), core, y) for i in range(1, NZ)],
        "y": [dev(x, z, core, lax.rem(y + i, ny)) for i in range(1, ny)],
    }
    return (x, z, core, y), peers


def greet_axes(peers):
    barrier = pltpu.get_barrier_semaphore()
    count = 0
    for axis in "cyxz":
        for peer in peers[axis]:
            pl.semaphore_signal(barrier, inc=1, device_id=peer, device_id_type=MESH)
            count += 1
    return barrier, count


def spread(pos, size, peers, source, target, ssem, rsem):
    def copy(i, send):
        p = lax.rem(pos + i, size)
        return pltpu.make_async_remote_copy(
            src_ref=source(p), dst_ref=target(pos if send else p),
            send_sem=ssem.at[p], recv_sem=rsem.at[pos if send else p],
            device_id=peers[i - 1], device_id_type=MESH,
        )

    for i in range(1, size):
        copy(i, True).start()

    def finish():
        for i in range(1, size):
            done = copy(i, False)
            done.wait_recv()
            done.wait_send()

    return finish


def block_inverse(d):
    n = d.shape[0]
    eye = (lax.broadcasted_iota(I32, (n, n), 0) == lax.broadcasted_iota(I32, (n, n), 1)).astype(F32)
    trace = jnp.sum(d * eye)
    widest = jnp.max(jnp.sum(jnp.abs(d), axis=1, keepdims=True))
    bound = jnp.minimum(trace, widest)
    low = 1.0 / bound
    inv = eye * (1.0 / bound)
    for _ in range(NEWTON_STEPS):
        inv = inv * (2.0 / (1.0 + low))
        left = jnp.dot(d, inv, precision=HI, preferred_element_type=F32)
        inv = 2.0 * inv - jnp.dot(inv, left, precision=HI, preferred_element_type=F32)
        low = 4.0 * low / ((1.0 + low) * (1.0 + low))
    return inv


def scores_kernel(tiles, parts, width, *refs):
    first_ref, scale_ref = refs[0], refs[1]
    groups = [refs[2 + 3 * g: 5 + 3 * g] for g in range(len(parts))]
    out_ref, sums_ref, con_ref = refs[2 + 3 * len(parts):]
    rows = groups[0][1].shape[1]
    sums_ref[...] = jnp.zeros_like(sums_ref)
    out_ref[...] = jnp.zeros_like(out_ref)
    cluster = lax.broadcasted_iota(I32, (width, rows), 0) + first_ref[0]

    for (start, count, base), (code_ref, x_ref, m_ref) in zip(parts, groups):
        def add(i, carry):
            spots, sums = [], []
            for u in range(UNROLL):
                a = start + UNROLL * i + u
                hot = jnp.where(cluster == m_ref[a][:, :rows], 1.0, 0.0).astype(BF16)
                sums.append(jnp.dot(hot, x_ref[UNROLL * i + u], preferred_element_type=F32))
                spots.append(code_ref[a, 0, rows] // tiles + base)
            for spot, part in zip(spots, sums):
                sums_ref[spot] += part
            return carry

        lax.fori_loop(0, count // UNROLL, add, 0)

    mine = scale_ref[:, pl.ds(pl.multiple_of(first_ref[0], width), width)]
    scale = jnp.broadcast_to(mine, (128, width)).T

    def normalise(b, carry):
        con_ref[b] = (sums_ref[b] * scale).astype(BF16)
        return carry

    lax.fori_loop(0, sums_ref.shape[0], normalise, 0)

    for (start, count, base), (code_ref, x_ref, m_ref) in zip(parts, groups):
        def score(i, carry):
            spots, values = [], []
            for u in range(UNROLL):
                a = start + UNROLL * i + u
                code = code_ref[a, 0, rows]
                values.append(dot_t(x_ref[UNROLL * i + u], con_ref[code // tiles + base]))
                spots.append((a, lax.rem(code, tiles)))
            for (a, tile), value in zip(spots, values):
                out_ref[a, tile] += value
            return carry

        lax.fori_loop(0, count // UNROLL, score, 0)


def partial_scores(tiles, width, first, scale, parts, arrays):
    n = arrays[0][2].shape[0]
    rows = arrays[0][1].shape[1]
    ny = K // width
    flat = [a for group in arrays for a in group]
    return pl.pallas_call(
        functools.partial(scores_kernel, tiles, parts, width),
        out_shape=jax.ShapeDtypeStruct((n, tiles, rows, width), F32),
        in_specs=[SMEM, VMEM] + [SMEM, VMEM, VMEM] * len(parts),
        out_specs=VMEM,
        scratch_shapes=[
            pltpu.VMEM((ny * BLK_OWN, width, 128), F32),
            pltpu.VMEM((ny * BLK_OWN, width, 128), BF16),
        ],
        compiler_params=params(),
        cost_estimate=cost(45),
        name="partial_scores",
    )(first, scale, *flat)


def gram_part(sums_ref, scale_ref, part):
    scale = jnp.broadcast_to(scale_ref[...], (128, K)).T
    part[...] = jnp.zeros_like(part)
    chunk = 4

    def step(i, carry):
        pieces = [(sums_ref[i * chunk + j] * scale).astype(BF16) for j in range(chunk)]
        c = jnp.concatenate(pieces, axis=1)
        part[...] += dot_t(c, c).reshape(part.shape)
        return carry

    lax.fori_loop(0, sums_ref.shape[0] // chunk, step, 0)


def inverse_panel(a_ref, p):
    n = 128
    cut = slice(p * n, (p + 1) * n)
    inv = block_inverse(a_ref[cut, cut])
    row = jnp.dot(inv, a_ref[cut, :], precision=HI, preferred_element_type=F32)
    col = a_ref[:, cut]
    for q in range(K // n):
        if q == p:
            continue
        rest = slice(q * n, (q + 1) * n)
        c = col[rest]
        a_ref[rest, :] -= jnp.dot(c, row, precision=HI, preferred_element_type=F32)
        a_ref[rest, cut] = -jnp.dot(c, inv, precision=HI, preferred_element_type=F32)
    a_ref[cut, :] = row
    a_ref[cut, cut] = inv


def reduce_kernel(ny, s_ref, sums_ref, scale_ref, scores_ref, a_ref,
                  rc, acc, rx, rn, rf, lsem,
                  part, gc, a1, gy, a2, gx, a3, gz, gram,
                  cs, cr, xs, xr, zs, zr, ys, yr,
                  gcs, gcr, gys, gyr, gxs, gxr, gzs, gzr,
                  gxs2, gxr2, gys2, gyr2, gcs2, gcr2):
    (x, z, core, y), peers = axis_peers(ny)
    barrier, count = greet_axes(peers)
    width = rc.shape[-1]
    order = [lax.rem(x + i, NX) for i in (NX - 1, 1, 2, 0)]
    own = []
    for i, p in enumerate(order):
        copy = pltpu.make_async_copy(s_ref.at[p, :, core], acc.at[p], lsem.at[i])
        copy.start()
        own.append(copy)
    pl.semaphore_wait(barrier, count)
    swap = []
    for i, p in enumerate(order):
        copy = pltpu.make_async_remote_copy(
            src_ref=s_ref.at[p, :, NC - 1 - core], dst_ref=rc.at[p],
            send_sem=cs.at[i], recv_sem=cr.at[i],
            device_id=peers["c"][0], device_id_type=MESH,
        )
        copy.start()
        swap.append(copy)

    def pair(i):
        own[i].wait()
        swap[i].wait_recv()
        acc[order[i]] += rc[order[i]]

    cut = NZ // 2
    upper, lower = peers["x"][0], peers["x"][NX - 2]

    def hop(s, down):
        sent = lax.rem(x + (s + 1 if down else 2 * NX - s - 1), NX)
        part_z = pl.ds(cut if down else 0, cut)
        return pltpu.make_async_remote_copy(
            src_ref=acc.at[sent, part_z], dst_ref=rx.at[s, part_z],
            send_sem=xs.at[2 * s + down], recv_sem=xr.at[2 * s + down],
            device_id=lower if down else upper, device_id_type=MESH,
        )

    def land(s, down):
        hop(s, down).wait_recv()
        got = lax.rem(x + (s + 2 if down else 2 * NX - s - 2), NX)
        part_z = pl.ds(cut if down else 0, cut)
        acc[got, part_z] += rx[s, part_z]

    docs = rc.shape[2]

    def ahead(side, reach):
        return lax.rem(z + (NZ - reach if side else reach), NZ)

    def part_d(side):
        return pl.ds(side * (docs // 2), docs // 2)

    def zcopy(source, target, sem, p):
        return pltpu.make_async_remote_copy(
            src_ref=source, dst_ref=target, send_sem=zs.at[sem], recv_sem=zr.at[sem],
            device_id=dev(x, p, core, y), device_id_type=MESH,
        )

    def far(side):
        return zcopy(acc.at[x, ahead(side, 3)], rf.at[side], side, ahead(side, 1))

    def fourth(side):
        return zcopy(acc.at[x, ahead(side, 4), part_d(side)], rf.at[2, part_d(side)],
                     2 + side, ahead(side, 2))

    def near(side, reach):
        slot = 2 * reach - 2 + side
        return zcopy(acc.at[x, ahead(side, reach)], rn.at[slot], 4 + slot, ahead(side, reach))

    blocks = part.shape[0]
    half = blocks // NC
    quarter = half // ny

    gram_part(sums_ref, scale_ref, part)
    finish = spread(core, NC, peers["c"],
                    lambda p: part.at[pl.ds(p * half, half)], lambda p: gc, gcs, gcr)
    pair(0)
    hop(0, 0).start()
    pair(1)
    hop(0, 1).start()
    finish()
    a1[...] = part[pl.ds(core * half, half)] + gc[...]
    finish = spread(y, ny, peers["y"],
                    lambda p: a1.at[pl.ds(p * quarter, quarter)], lambda p: gy.at[p], gys, gyr)
    pair(2)
    pair(3)
    gy[y] = a1[pl.ds(y * quarter, quarter)]
    finish()
    total = gy[0]
    for i in range(1, ny):
        total = total + gy[i]
    a2[...] = total
    finish = spread(x, NX, peers["x"], lambda p: a2.at[p], lambda p: gx.at[p], gxs, gxr)
    gx[x] = a2[x]
    for down in range(2):
        land(0, down)
        hop(1, down).start()
    finish()
    total = gx[0]
    for i in range(1, NX):
        total = total + gx[i]
    a3[...] = total
    gz[z] = total
    spread(z, NZ, peers["z"], lambda p: a3, lambda p: gz.at[p], gzs, gzr)()
    total = gz[0]
    for i in range(1, NZ):
        total = total + gz[i]
    base = core * half + y * quarter
    gram[base + x] = total
    finish = spread(x, NX, peers["x"], lambda p: gram.at[base + x],
                    lambda p: gram.at[base + p], gxs2, gxr2)
    for down in range(2):
        land(1, down)
        hop(2, down).start()
    finish()
    finish = spread(y, ny, peers["y"], lambda p: gram.at[pl.ds(base, quarter)],
                    lambda p: gram.at[pl.ds(core * half + p * quarter, quarter)], gys2, gyr2)
    for down in range(2):
        land(2, down)
    for side in range(2):
        far(side).start()
        fourth(side).start()
    for side in range(2):
        near(side, 1).start()
    finish()
    spread(core, NC, peers["c"], lambda p: gram.at[pl.ds(core * half, half)],
           lambda p: gram.at[pl.ds(p * half, half)], gcs2, gcr2)()

    eye = (lax.broadcasted_iota(I32, (K, K), 0) == lax.broadcasted_iota(I32, (K, K), 1)).astype(F32)
    a_ref[...] = gram[...].reshape(K, K) + RIDGE_WEIGHT * eye
    inverse_panel(a_ref, 0)
    for side in range(2):
        far(side).wait_recv()
        fourth(side).wait_recv()
        p = ahead(side, 2)
        acc[x, p] += rf[side]
        acc[x, p, part_d(side)] += rf[2, part_d(side)]
        near(side, 2).start()
    inverse_panel(a_ref, 1)
    inverse_panel(a_ref, 2)
    total = acc[x, z]
    for side in range(2):
        for reach in range(1, 3):
            near(side, reach).wait_recv()
            total = total + rn[2 * reach - 2 + side]

    def lanes(p):
        return pl.ds(pl.multiple_of(p * width, width), width)

    scores_ref[:, lanes(y)] = total
    finish = spread(y, ny, peers["y"], lambda p: scores_ref.at[:, lanes(y)],
                    lambda p: scores_ref.at[:, lanes(p)], ys, yr)
    inverse_panel(a_ref, 3)
    finish()
    for side in range(2):
        for copy in (far(side), fourth(side), near(side, 1), near(side, 2)):
            copy.wait_send()
    for copy in swap:
        copy.wait_send()
    for s in range(NX - 1):
        for down in range(2):
            hop(s, down).wait_send()


def reduce_scores(ny, partial, sums, scale):
    n, tiles, rows, width = partial.shape
    docs = tiles * rows
    part_rows = K // (NC * ny * NX)
    blocks = K // part_rows
    half, quarter = blocks // NC, blocks // (NC * ny)
    sems = []
    for size in (NX, 2 * (NX - 1), NZ, ny, NC, ny, NX, NZ, NX, ny, NC):
        sems += [DMA((size,)), DMA((size,))]
    return pl.pallas_call(
        functools.partial(reduce_kernel, ny),
        out_shape=(jax.ShapeDtypeStruct((docs, K), F32), jax.ShapeDtypeStruct((K, K), F32)),
        in_specs=[ANY, VMEM, VMEM],
        out_specs=(VMEM, VMEM),
        scratch_shapes=[
            pltpu.VMEM((NX, NZ, docs, width), F32),
            pltpu.VMEM((NX, NZ, docs, width), F32),
            pltpu.VMEM((NX - 1, NZ, docs, width), F32),
            pltpu.VMEM((4, docs, width), F32),
            pltpu.VMEM((3, docs, width), F32),
            DMA((NX,)),
            pltpu.VMEM((blocks, part_rows, K), F32),
            pltpu.VMEM((half, part_rows, K), F32),
            pltpu.VMEM((half, part_rows, K), F32),
            pltpu.VMEM((ny, quarter, part_rows, K), F32),
            pltpu.VMEM((quarter, part_rows, K), F32),
            pltpu.VMEM((NX, part_rows, K), F32),
            pltpu.VMEM((part_rows, K), F32),
            pltpu.VMEM((NZ, part_rows, K), F32),
            pltpu.VMEM((blocks, part_rows, K), F32),
        ] + sems,
        compiler_params=params(2),
        name="reduce_scores",
    )(partial.reshape(NX, NZ, NC, docs, width), sums, scale)


def shift(array, ny, by):
    return lax.ppermute(array, "terms", [(i, (i + by) % ny) for i in range(ny)])


def body(values, block_ids, assignment):
    tiles, slots, rows, block_width = values.shape
    ny = lax.axis_size("terms")
    pairs = tiles * slots
    width = K // ny
    y = lax.axis_index("terms")
    labels = jnp.pad(
        assignment.reshape(tiles, 1, rows), ((0, 0), (0, 0), (0, 128 - rows)), constant_values=-1
    )
    ordered, meta = order_blocks(
        values.reshape(pairs, rows, block_width), block_ids, labels
    )
    own_x, own_m = exchange(ordered, meta)

    half = pairs // 2
    arrays, parts = [(own_m, own_x, own_m)], [(0, pairs, 0)]
    up_x, down_x = shift(own_x, ny, 1), shift(own_x, ny, -1)
    up_m = shift(own_m, ny, 1)
    arrays.append((up_m, up_x, up_m))
    parts.append((0, pairs, BLK_OWN))
    if ny > 2:
        down_m, far_m = shift(own_m, ny, -1), shift(own_m, ny, 2)
        far_a = shift(up_x[:half], ny, 1)
        far_b = shift(down_x[half:], ny, -1)
        arrays.append((down_m, down_x, down_m))
        parts.append((0, pairs, 3 * BLK_OWN))
        arrays.append((far_m, far_a, far_m))
        parts.append((0, half, 2 * BLK_OWN))
        arrays.append((far_m, far_b, far_m))
        parts.append((half, half, 2 * BLK_OWN))

    sums, sq = own_sums(tiles, own_m, own_x, own_m)
    scale = norm_scale(ny, sq)
    first = (y * width).reshape(1)
    partial = partial_scores(tiles, width, first, scale, tuple(parts), arrays)
    scores, inverse = reduce_scores(ny, partial, sums, scale)
    inverse_cols = lax.dynamic_slice_in_dim(inverse, y * width, width, 1)
    return jnp.dot(scores, inverse_cols, precision=HI, preferred_element_type=F32)


def solution(mesh):
    in_specs = (P("docs", "terms", None, None), P("docs", "terms"), P("docs", None))
    out_specs = P("docs", "terms")
    return jax.shard_map(body, mesh=mesh, in_specs=in_specs, out_specs=out_specs, check_vma=False)
```

```python
import functools

import jax
import jax.numpy as jnp
from jax import lax
from jax.experimental import pallas as pl
from jax.experimental.pallas import tpu as pltpu
from jax.sharding import PartitionSpec as P

K = 512
BLK_OWN = 32
NX = 4
NZ = 8
NC = 2
EPSILON = 1e-06
RIDGE_WEIGHT = 1.0
NEWTON_STEPS = 8
UNROLL = 8

F32 = jnp.float32
BF16 = jnp.bfloat16
I32 = jnp.int32
MESH = pl.DeviceIdType.MESH
HI = lax.Precision.HIGHEST
VMEM = pl.BlockSpec(memory_space=pltpu.VMEM)
SMEM = pl.BlockSpec(memory_space=pltpu.SMEM)
ANY = pl.BlockSpec(memory_space=pl.ANY)
DMA = pltpu.SemaphoreType.DMA
VLIM = 60 * 1024 * 1024


def dot_t(a, b, precision=None):
    return lax.dot_general(
        a, b, (((1,), (1,)), ((), ())), precision=precision, preferred_element_type=F32
    )


def coords():
    d = lax.axis_index("docs")
    core = lax.rem(d, NC)
    chip = d // NC
    return chip // NZ, lax.rem(chip, NZ), core, lax.axis_index("terms")


def dev(x, z, core, y):
    return {"docs": (x * NZ + z) * NC + core, "terms": y}


def cost(us):
    return pl.CostEstimate(flops=int(us * 5e8), bytes_accessed=int(us * 2e6), transcendentals=0)


def params(collective_id=None):
    return pltpu.CompilerParams(
        collective_id=collective_id,
        has_side_effects=collective_id is not None,
        vmem_limit_bytes=VLIM,
    )


def order_kernel(ids_ref, v_ref, lab_ref, x_ref, m_ref, c_ref):
    pairs = v_ref.shape[0]
    slots = pairs // lab_ref.shape[0]
    lane = lax.broadcasted_iota(I32, (1, 128), 1)

    def step(p, carry):
        block = ids_ref[p // slots, lax.rem(p, slots)]
        owner = block // BLK_OWN
        tile = p // slots
        code = lax.rem(block, BLK_OWN) * lab_ref.shape[0] + tile
        x_ref[owner] = v_ref[p]
        m_ref[owner] = jnp.where(lane == 64, code, lab_ref[tile])
        return carry

    lax.fori_loop(0, pairs, step, 0)


def order_blocks(values, ids, labels):
    pairs = values.shape[0]

    def kernel(ids_ref, v_ref, lab_ref, x_ref, m_ref):
        order_kernel(ids_ref, v_ref, lab_ref, x_ref, m_ref, None)

    return pl.pallas_call(
        kernel,
        out_shape=(
            jax.ShapeDtypeStruct(values.shape, BF16),
            jax.ShapeDtypeStruct((pairs, 1, 128), I32),
        ),
        in_specs=[SMEM, VMEM, VMEM],
        out_specs=(VMEM, VMEM),
        compiler_params=params(),
        name="order_blocks",
    )(ids, values, labels)


def exchange_kernel(x_ref, m_ref, ox_ref, om_ref, sx, rx, sm, rm, lsem):
    n = x_ref.shape[0]
    me = lax.axis_index("docs")
    barrier = pltpu.get_barrier_semaphore()

    def greet(i, carry):
        peer = lax.rem(me + i, n)
        pl.semaphore_signal(barrier, inc=1, device_id={"docs": peer}, device_id_type=MESH)
        return carry

    lax.fori_loop(1, n, greet, 0)
    own_x = pltpu.make_async_copy(x_ref.at[me], ox_ref.at[me], lsem.at[0])
    own_m = pltpu.make_async_copy(m_ref.at[me], om_ref.at[me], lsem.at[1])
    own_x.start()
    own_m.start()
    pl.semaphore_wait(barrier, n - 1)

    def copies(peer, slot):
        one = pltpu.make_async_remote_copy(
            src_ref=x_ref.at[peer], dst_ref=ox_ref.at[slot],
            send_sem=sx.at[peer], recv_sem=rx.at[slot],
            device_id={"docs": peer}, device_id_type=MESH,
        )
        two = pltpu.make_async_remote_copy(
            src_ref=m_ref.at[peer], dst_ref=om_ref.at[slot],
            send_sem=sm.at[peer], recv_sem=rm.at[slot],
            device_id={"docs": peer}, device_id_type=MESH,
        )
        return one, two

    def send(i, carry):
        one, two = copies(lax.rem(me + i, n), me)
        two.start()
        one.start()
        return carry

    lax.fori_loop(1, n, send, 0)
    own_x.wait()
    own_m.wait()

    def finish(i, carry):
        peer = lax.rem(me + i, n)
        one, two = copies(peer, peer)
        one.wait_recv()
        two.wait_recv()
        one.wait_send()
        two.wait_send()
        return carry

    lax.fori_loop(1, n, finish, 0)


def exchange(x, m):
    n = x.shape[0]
    return pl.pallas_call(
        exchange_kernel,
        out_shape=(jax.ShapeDtypeStruct(x.shape, x.dtype), jax.ShapeDtypeStruct(m.shape, m.dtype)),
        in_specs=[VMEM, VMEM],
        out_specs=(VMEM, VMEM),
        scratch_shapes=[DMA((n,)), DMA((n,)), DMA((n,)), DMA((n,)), DMA((2,))],
        compiler_params=params(0),
        name="exchange_blocks",
    )(x, m)


def sums_kernel(tiles, code_ref, x_ref, m_ref, sums_ref, sq_ref):
    n, rows, _ = x_ref.shape
    sums_ref[...] = jnp.zeros_like(sums_ref)
    cluster = lax.broadcasted_iota(I32, (K, rows), 0)

    def step(i, carry):
        spots, sums = [], []
        for u in range(4):
            a = 4 * i + u
            hot = jnp.where(cluster == m_ref[a][:, :rows], 1.0, 0.0).astype(BF16)
            sums.append(jnp.dot(hot, x_ref[a], preferred_element_type=F32))
            spots.append(code_ref[a, 0, rows] // tiles)
        for spot, part in zip(spots, sums):
            sums_ref[spot] += part
        return carry

    lax.fori_loop(0, n // 4, step, 0)

    def square(c, total):
        s = sums_ref[c]
        return total + s * s

    total = lax.fori_loop(0, sums_ref.shape[0], square, jnp.zeros((K, 128), F32))
    sq_ref[...] = dot_t(jnp.ones((8, 128), F32), total, HI)[:1]


def own_sums(tiles, code, x, m):
    return pl.pallas_call(
        functools.partial(sums_kernel, tiles),
        out_shape=(
            jax.ShapeDtypeStruct((BLK_OWN, K, 128), F32),
            jax.ShapeDtypeStruct((1, K), F32),
        ),
        in_specs=[SMEM, VMEM, VMEM],
        out_specs=(VMEM, VMEM),
        compiler_params=params(),
        cost_estimate=cost(17),
        name="own_sums",
    )(code, x, m)


def norm_kernel(ny, sq_ref, scale_ref, slots, zslots, stage, ssem, rsem, zssem, zrsem):
    x, z, core, y = coords()
    group = NX * ny * NC
    me = (x * ny + y) * NC + core
    barrier = pltpu.get_barrier_semaphore()

    def member(g):
        return dev(g // (ny * NC), z, lax.rem(g, NC), lax.rem(g // NC, ny))

    def greet(i, carry):
        pl.semaphore_signal(
            barrier, inc=1, device_id=member(lax.rem(me + i, group)), device_id_type=MESH
        )
        return carry

    lax.fori_loop(1, group, greet, 0)
    for i in range(1, NZ):
        pl.semaphore_signal(
            barrier, inc=1, device_id=dev(x, lax.rem(z + i, NZ), core, y), device_id_type=MESH
        )
    slots[me] = sq_ref[...]
    pl.semaphore_wait(barrier, group - 1 + NZ - 1)

    def copy(peer, slot):
        return pltpu.make_async_remote_copy(
            src_ref=sq_ref, dst_ref=slots.at[slot],
            send_sem=ssem.at[peer], recv_sem=rsem.at[slot],
            device_id=member(peer), device_id_type=MESH,
        )

    def send(i, carry):
        copy(lax.rem(me + i, group), me).start()
        return carry

    lax.fori_loop(1, group, send, 0)

    def finish(i, carry):
        peer = lax.rem(me + i, group)
        done = copy(peer, peer)
        done.wait_recv()
        done.wait_send()
        return carry

    lax.fori_loop(1, group, finish, 0)
    total = jnp.sum(slots[...], axis=0)
    stage[...] = total
    zslots[z] = total

    def zcopy(peer, slot):
        return pltpu.make_async_remote_copy(
            src_ref=stage, dst_ref=zslots.at[slot],
            send_sem=zssem.at[peer], recv_sem=zrsem.at[slot],
            device_id=dev(x, peer, core, y), device_id_type=MESH,
        )

    for i in range(1, NZ):
        zcopy(lax.rem(z + i, NZ), z).start()
    for i in range(1, NZ):
        peer = lax.rem(z + i, NZ)
        done = zcopy(peer, peer)
        done.wait_recv()
        done.wait_send()
    scale_ref[...] = lax.rsqrt(jnp.sum(zslots[...], axis=0) + EPSILON)


def norm_scale(ny, sq):
    group = NX * ny * NC
    return pl.pallas_call(
        functools.partial(norm_kernel, ny),
        out_shape=jax.ShapeDtypeStruct((1, K), F32),
        in_specs=[VMEM],
        out_specs=VMEM,
        scratch_shapes=[
            pltpu.VMEM((group, 1, K), F32),
            pltpu.VMEM((NZ, 1, K), F32),
            pltpu.VMEM((1, K), F32),
            DMA((group,)), DMA((group,)), DMA((NZ,)), DMA((NZ,)),
        ],
        compiler_params=params(1),
        cost_estimate=cost(17),
        name="norm_scale",
    )(sq)


def axis_peers(ny):
    x, z, core, y = coords()
    peers = {
        "c": [dev(x, z, lax.rem(core + i, NC), y) for i in range(1, NC)],
        "x": [dev(lax.rem(x + i, NX), z, core, y) for i in range(1, NX)],
        "z": [dev(x, lax.rem(z + i, NZ), core, y) for i in range(1, NZ)],
        "y": [dev(x, z, core, lax.rem(y + i, ny)) for i in range(1, ny)],
    }
    return (x, z, core, y), peers


def greet_axes(peers):
    barrier = pltpu.get_barrier_semaphore()
    count = 0
    for axis in "cyxz":
        for peer in peers[axis]:
            pl.semaphore_signal(barrier, inc=1, device_id=peer, device_id_type=MESH)
            count += 1
    return barrier, count


def spread(pos, size, peers, source, target, ssem, rsem):
    def copy(i, send):
        p = lax.rem(pos + i, size)
        return pltpu.make_async_remote_copy(
            src_ref=source(p), dst_ref=target(pos if send else p),
            send_sem=ssem.at[p], recv_sem=rsem.at[pos if send else p],
            device_id=peers[i - 1], device_id_type=MESH,
        )

    for i in range(1, size):
        copy(i, True).start()

    def finish():
        for i in range(1, size):
            done = copy(i, False)
            done.wait_recv()
            done.wait_send()

    return finish


def block_inverse(d):
    n = d.shape[0]
    eye = (lax.broadcasted_iota(I32, (n, n), 0) == lax.broadcasted_iota(I32, (n, n), 1)).astype(F32)
    trace = jnp.sum(d * eye)
    widest = jnp.max(jnp.sum(jnp.abs(d), axis=1, keepdims=True))
    bound = jnp.minimum(trace, widest)
    low = 1.0 / bound
    inv = eye * (1.0 / bound)
    for _ in range(NEWTON_STEPS):
        inv = inv * (2.0 / (1.0 + low))
        left = jnp.dot(d, inv, precision=HI, preferred_element_type=F32)
        inv = 2.0 * inv - jnp.dot(inv, left, precision=HI, preferred_element_type=F32)
        low = 4.0 * low / ((1.0 + low) * (1.0 + low))
    return inv


def scores_kernel(tiles, parts, width, *refs):
    first_ref, scale_ref = refs[0], refs[1]
    groups = [refs[2 + 3 * g: 5 + 3 * g] for g in range(len(parts))]
    out_ref, sums_ref, con_ref = refs[2 + 3 * len(parts):]
    rows = groups[0][1].shape[1]
    sums_ref[...] = jnp.zeros_like(sums_ref)
    out_ref[...] = jnp.zeros_like(out_ref)
    cluster = lax.broadcasted_iota(I32, (width, rows), 0) + first_ref[0]

    for (start, count, base), (code_ref, x_ref, m_ref) in zip(parts, groups):
        def add(i, carry):
            spots, sums = [], []
            for u in range(UNROLL):
                a = start + UNROLL * i + u
                hot = jnp.where(cluster == m_ref[a][:, :rows], 1.0, 0.0).astype(BF16)
                sums.append(jnp.dot(hot, x_ref[UNROLL * i + u], preferred_element_type=F32))
                spots.append(code_ref[a, 0, rows] // tiles + base)
            for spot, part in zip(spots, sums):
                sums_ref[spot] += part
            return carry

        lax.fori_loop(0, count // UNROLL, add, 0)

    mine = scale_ref[:, pl.ds(pl.multiple_of(first_ref[0], width), width)]
    scale = jnp.broadcast_to(mine, (128, width)).T

    def normalise(b, carry):
        con_ref[b] = (sums_ref[b] * scale).astype(BF16)
        return carry

    lax.fori_loop(0, sums_ref.shape[0], normalise, 0)

    for (start, count, base), (code_ref, x_ref, m_ref) in zip(parts, groups):
        def score(i, carry):
            spots, values = [], []
            for u in range(UNROLL):
                a = start + UNROLL * i + u
                code = code_ref[a, 0, rows]
                values.append(dot_t(x_ref[UNROLL * i + u], con_ref[code // tiles + base]))
                spots.append((a, lax.rem(code, tiles)))
            for (a, tile), value in zip(spots, values):
                out_ref[a, tile] += value
            return carry

        lax.fori_loop(0, count // UNROLL, score, 0)


def partial_scores(tiles, width, first, scale, parts, arrays):
    n = arrays[0][2].shape[0]
    rows = arrays[0][1].shape[1]
    ny = K // width
    flat = [a for group in arrays for a in group]
    return pl.pallas_call(
        functools.partial(scores_kernel, tiles, parts, width),
        out_shape=jax.ShapeDtypeStruct((n, tiles, rows, width), F32),
        in_specs=[SMEM, VMEM] + [SMEM, VMEM, VMEM] * len(parts),
        out_specs=VMEM,
        scratch_shapes=[
            pltpu.VMEM((ny * BLK_OWN, width, 128), F32),
            pltpu.VMEM((ny * BLK_OWN, width, 128), BF16),
        ],
        compiler_params=params(),
        cost_estimate=cost(45),
        name="partial_scores",
    )(first, scale, *flat)


def gram_part(sums_ref, scale_ref, part):
    scale = jnp.broadcast_to(scale_ref[...], (128, K)).T
    part[...] = jnp.zeros_like(part)
    chunk = 4

    def step(i, carry):
        pieces = [(sums_ref[i * chunk + j] * scale).astype(BF16) for j in range(chunk)]
        c = jnp.concatenate(pieces, axis=1)
        part[...] += dot_t(c, c).reshape(part.shape)
        return carry

    lax.fori_loop(0, sums_ref.shape[0] // chunk, step, 0)


def inverse_panel(a_ref, p):
    n = 128
    cut = slice(p * n, (p + 1) * n)
    inv = block_inverse(a_ref[cut, cut])
    row = jnp.dot(inv, a_ref[cut, :], precision=HI, preferred_element_type=F32)
    col = a_ref[:, cut]
    for q in range(K // n):
        if q == p:
            continue
        rest = slice(q * n, (q + 1) * n)
        c = col[rest]
        a_ref[rest, :] -= jnp.dot(c, row, precision=HI, preferred_element_type=F32)
        a_ref[rest, cut] = -jnp.dot(c, inv, precision=HI, preferred_element_type=F32)
    a_ref[cut, :] = row
    a_ref[cut, cut] = inv


def reduce_kernel(ny, s_ref, sums_hbm, scale_ref, scores_ref, a_ref,
                  rc, acc, rx, rn, rf, lsem, sums_ref,
                  part, gc, a1, gy, a2, gx, a3, gz, gram,
                  cs, cr, xs, xr, zs, zr, ys, yr,
                  gcs, gcr, gys, gyr, gxs, gxr, gzs, gzr,
                  gxs2, gxr2, gys2, gyr2, gcs2, gcr2):
    (x, z, core, y), peers = axis_peers(ny)
    barrier, count = greet_axes(peers)
    width = rc.shape[-1]
    order = [lax.rem(x + i, NX) for i in (NX - 1, 1, 2, 0)]
    load = pltpu.make_async_copy(sums_hbm, sums_ref, lsem.at[NX])
    load.start()
    own = []
    for i, p in enumerate(order):
        copy = pltpu.make_async_copy(s_ref.at[p, :, core], acc.at[p], lsem.at[i])
        copy.start()
        own.append(copy)
    pl.semaphore_wait(barrier, count)
    swap = []
    for i, p in enumerate(order):
        copy = pltpu.make_async_remote_copy(
            src_ref=s_ref.at[p, :, NC - 1 - core], dst_ref=rc.at[p],
            send_sem=cs.at[i], recv_sem=cr.at[i],
            device_id=peers["c"][0], device_id_type=MESH,
        )
        copy.start()
        swap.append(copy)

    def pair(i):
        own[i].wait()
        swap[i].wait_recv()
        acc[order[i]] += rc[order[i]]

    cut = NZ // 2
    upper, lower = peers["x"][0], peers["x"][NX - 2]

    def hop(s, down, sub):
        sent = lax.rem(x + (s + 1 if down else 2 * NX - s - 1), NX)
        part_z = pl.ds(down * cut + sub * (cut // 2), cut // 2)
        sem = 4 * s + 2 * down + sub
        return pltpu.make_async_remote_copy(
            src_ref=acc.at[sent, part_z], dst_ref=rx.at[s, part_z],
            send_sem=xs.at[sem], recv_sem=xr.at[sem],
            device_id=lower if down else upper, device_id_type=MESH,
        )

    def land(s, sub):
        for down in range(2):
            hop(s, down, sub).wait_recv()
            got = lax.rem(x + (s + 2 if down else 2 * NX - s - 2), NX)
            part_z = pl.ds(down * cut + sub * (cut // 2), cut // 2)
            acc[got, part_z] += rx[s, part_z]

    def go(s, sub):
        for down in range(2):
            hop(s, down, sub).start()

    docs = rc.shape[2]

    def ahead(side, reach):
        return lax.rem(z + (NZ - reach if side else reach), NZ)

    def part_d(side):
        return pl.ds(side * (docs // 2), docs // 2)

    def zcopy(source, target, sem, p):
        return pltpu.make_async_remote_copy(
            src_ref=source, dst_ref=target, send_sem=zs.at[sem], recv_sem=zr.at[sem],
            device_id=dev(x, p, core, y), device_id_type=MESH,
        )

    def far(side):
        return zcopy(acc.at[x, ahead(side, 3)], rf.at[side], side, ahead(side, 1))

    def fourth(side):
        return zcopy(acc.at[x, ahead(side, 4), part_d(side)], rf.at[2, part_d(side)],
                     2 + side, ahead(side, 2))

    def near(side, reach):
        slot = 2 * reach - 2 + side
        return zcopy(acc.at[x, ahead(side, reach)], rn.at[slot], 4 + slot, ahead(side, reach))

    blocks = part.shape[0]
    half = blocks // NC
    quarter = half // ny

    load.wait()
    gram_part(sums_ref, scale_ref, part)
    finish = spread(core, NC, peers["c"],
                    lambda p: part.at[pl.ds(p * half, half)], lambda p: gc, gcs, gcr)
    pair(0)
    for sub in range(2):
        hop(0, 0, sub).start()
    pair(1)
    for sub in range(2):
        hop(0, 1, sub).start()
    finish()
    a1[...] = part[pl.ds(core * half, half)] + gc[...]
    finish = spread(y, ny, peers["y"],
                    lambda p: a1.at[pl.ds(p * quarter, quarter)], lambda p: gy.at[p], gys, gyr)
    pair(2)
    pair(3)
    gy[y] = a1[pl.ds(y * quarter, quarter)]
    finish()
    total = gy[0]
    for i in range(1, ny):
        total = total + gy[i]
    a2[...] = total
    finish = spread(x, NX, peers["x"], lambda p: a2.at[p], lambda p: gx.at[p], gxs, gxr)
    gx[x] = a2[x]
    land(0, 0)
    go(1, 0)
    finish()
    total = gx[0]
    for i in range(1, NX):
        total = total + gx[i]
    a3[...] = total
    gz[z] = total
    finish = spread(z, NZ, peers["z"], lambda p: a3, lambda p: gz.at[p], gzs, gzr)
    land(0, 1)
    finish()
    total = gz[0]
    for i in range(1, NZ):
        total = total + gz[i]
    base = core * half + y * quarter
    gram[base + x] = total
    finish = spread(x, NX, peers["x"], lambda p: gram.at[base + x],
                    lambda p: gram.at[base + p], gxs2, gxr2)
    go(1, 1)
    land(1, 0)
    go(2, 0)
    finish()
    finish = spread(y, ny, peers["y"], lambda p: gram.at[pl.ds(base, quarter)],
                    lambda p: gram.at[pl.ds(core * half + p * quarter, quarter)], gys2, gyr2)
    finish()
    spread(core, NC, peers["c"], lambda p: gram.at[pl.ds(core * half, half)],
           lambda p: gram.at[pl.ds(p * half, half)], gcs2, gcr2)()
    land(1, 1)
    go(2, 1)

    eye = (lax.broadcasted_iota(I32, (K, K), 0) == lax.broadcasted_iota(I32, (K, K), 1)).astype(F32)
    a_ref[...] = gram[...].reshape(K, K) + RIDGE_WEIGHT * eye
    inverse_panel(a_ref, 0)
    land(2, 0)
    land(2, 1)
    for side in range(2):
        far(side).start()
        fourth(side).start()
    for side in range(2):
        near(side, 1).start()
    inverse_panel(a_ref, 1)
    for side in range(2):
        far(side).wait_recv()
        fourth(side).wait_recv()
        p = ahead(side, 2)
        acc[x, p] += rf[side]
        acc[x, p, part_d(side)] += rf[2, part_d(side)]
        near(side, 2).start()
    inverse_panel(a_ref, 2)
    total = acc[x, z]
    for side in range(2):
        for reach in range(1, 3):
            near(side, reach).wait_recv()
            total = total + rn[2 * reach - 2 + side]

    def lanes(p):
        return pl.ds(pl.multiple_of(p * width, width), width)

    scores_ref[:, lanes(y)] = total
    finish = spread(y, ny, peers["y"], lambda p: scores_ref.at[:, lanes(y)],
                    lambda p: scores_ref.at[:, lanes(p)], ys, yr)
    inverse_panel(a_ref, 3)
    finish()
    for side in range(2):
        for copy in (far(side), fourth(side), near(side, 1), near(side, 2)):
            copy.wait_send()
    for copy in swap:
        copy.wait_send()
    for s in range(NX - 1):
        for down in range(2):
            for sub in range(2):
                hop(s, down, sub).wait_send()


def reduce_scores(ny, partial, sums, scale):
    n, tiles, rows, width = partial.shape
    docs = tiles * rows
    part_rows = K // (NC * ny * NX)
    blocks = K // part_rows
    half, quarter = blocks // NC, blocks // (NC * ny)
    sems = []
    for size in (NX, 4 * (NX - 1), NZ, ny, NC, ny, NX, NZ, NX, ny, NC):
        sems += [DMA((size,)), DMA((size,))]
    return pl.pallas_call(
        functools.partial(reduce_kernel, ny),
        out_shape=(jax.ShapeDtypeStruct((docs, K), F32), jax.ShapeDtypeStruct((K, K), F32)),
        in_specs=[ANY, ANY, VMEM],
        out_specs=(VMEM, VMEM),
        scratch_shapes=[
            pltpu.VMEM((NX, NZ, docs, width), F32),
            pltpu.VMEM((NX, NZ, docs, width), F32),
            pltpu.VMEM((NX - 1, NZ, docs, width), F32),
            pltpu.VMEM((4, docs, width), F32),
            pltpu.VMEM((3, docs, width), F32),
            DMA((NX + 1,)),
            pltpu.VMEM(sums.shape, F32),
            pltpu.VMEM((blocks, part_rows, K), F32),
            pltpu.VMEM((half, part_rows, K), F32),
            pltpu.VMEM((half, part_rows, K), F32),
            pltpu.VMEM((ny, quarter, part_rows, K), F32),
            pltpu.VMEM((quarter, part_rows, K), F32),
            pltpu.VMEM((NX, part_rows, K), F32),
            pltpu.VMEM((part_rows, K), F32),
            pltpu.VMEM((NZ, part_rows, K), F32),
            pltpu.VMEM((blocks, part_rows, K), F32),
        ] + sems,
        compiler_params=params(2),
        name="reduce_scores",
    )(partial.reshape(NX, NZ, NC, docs, width), sums, scale)


def shift(array, ny, by):
    return lax.ppermute(array, "terms", [(i, (i + by) % ny) for i in range(ny)])


def body(values, block_ids, assignment):
    tiles, slots, rows, block_width = values.shape
    ny = lax.axis_size("terms")
    pairs = tiles * slots
    width = K // ny
    y = lax.axis_index("terms")
    labels = jnp.pad(
        assignment.reshape(tiles, 1, rows), ((0, 0), (0, 0), (0, 128 - rows)), constant_values=-1
    )
    ordered, meta = order_blocks(
        values.reshape(pairs, rows, block_width), block_ids, labels
    )
    own_x, own_m = exchange(ordered, meta)

    half = pairs // 2
    arrays, parts = [(own_m, own_x, own_m)], [(0, pairs, 0)]
    up_x, down_x = shift(own_x, ny, 1), shift(own_x, ny, -1)
    up_m = shift(own_m, ny, 1)
    arrays.append((up_m, up_x, up_m))
    parts.append((0, pairs, BLK_OWN))
    if ny > 2:
        down_m, far_m = shift(own_m, ny, -1), shift(own_m, ny, 2)
        far_a = shift(up_x[:half], ny, 1)
        far_b = shift(down_x[half:], ny, -1)
        arrays.append((down_m, down_x, down_m))
        parts.append((0, pairs, 3 * BLK_OWN))
        arrays.append((far_m, far_a, far_m))
        parts.append((0, half, 2 * BLK_OWN))
        arrays.append((far_m, far_b, far_m))
        parts.append((half, half, 2 * BLK_OWN))

    sums, sq = own_sums(tiles, own_m, own_x, own_m)
    scale = norm_scale(ny, sq)
    first = (y * width).reshape(1)
    partial = partial_scores(tiles, width, first, scale, tuple(parts), arrays)
    scores, inverse = reduce_scores(ny, partial, sums, scale)
    inverse_cols = lax.dynamic_slice_in_dim(inverse, y * width, width, 1)
    return jnp.dot(scores, inverse_cols, precision=HI, preferred_element_type=F32)


def solution(mesh):
    in_specs = (P("docs", "terms", None, None), P("docs", "terms"), P("docs", None))
    out_specs = P("docs", "terms")
    return jax.shard_map(body, mesh=mesh, in_specs=in_specs, out_specs=out_specs, check_vma=False)
```

```python
import functools

import jax
import jax.numpy as jnp
from jax import lax
from jax.experimental import pallas as pl
from jax.experimental.pallas import tpu as pltpu
from jax.sharding import PartitionSpec as P

K = 512
BLK_OWN = 32
NX = 4
NZ = 8
NC = 2
EPSILON = 1e-06
RIDGE_WEIGHT = 1.0
NEWTON_STEPS = 8
UNROLL = 8

F32 = jnp.float32
BF16 = jnp.bfloat16
I32 = jnp.int32
MESH = pl.DeviceIdType.MESH
HI = lax.Precision.HIGHEST
VMEM = pl.BlockSpec(memory_space=pltpu.VMEM)
SMEM = pl.BlockSpec(memory_space=pltpu.SMEM)
ANY = pl.BlockSpec(memory_space=pl.ANY)
DMA = pltpu.SemaphoreType.DMA
VLIM = 60 * 1024 * 1024


def dot_t(a, b, precision=None):
    return lax.dot_general(
        a, b, (((1,), (1,)), ((), ())), precision=precision, preferred_element_type=F32
    )


def coords():
    d = lax.axis_index("docs")
    core = lax.rem(d, NC)
    chip = d // NC
    return chip // NZ, lax.rem(chip, NZ), core, lax.axis_index("terms")


def dev(x, z, core, y):
    return {"docs": (x * NZ + z) * NC + core, "terms": y}


def cost(us):
    return pl.CostEstimate(flops=int(us * 5e8), bytes_accessed=int(us * 2e6), transcendentals=0)


def params(collective_id=None):
    return pltpu.CompilerParams(
        collective_id=collective_id,
        has_side_effects=collective_id is not None,
        vmem_limit_bytes=VLIM,
    )


def order_kernel(ids_ref, v_ref, lab_ref, x_ref, m_ref, c_ref):
    pairs = v_ref.shape[0]
    slots = pairs // lab_ref.shape[0]
    lane = lax.broadcasted_iota(I32, (1, 128), 1)

    def step(p, carry):
        block = ids_ref[p // slots, lax.rem(p, slots)]
        owner = block // BLK_OWN
        tile = p // slots
        code = lax.rem(block, BLK_OWN) * lab_ref.shape[0] + tile
        x_ref[owner] = v_ref[p]
        m_ref[owner] = jnp.where(lane == 64, code, lab_ref[tile])
        return carry

    lax.fori_loop(0, pairs, step, 0)


def order_blocks(values, ids, labels):
    pairs = values.shape[0]

    def kernel(ids_ref, v_ref, lab_ref, x_ref, m_ref):
        order_kernel(ids_ref, v_ref, lab_ref, x_ref, m_ref, None)

    return pl.pallas_call(
        kernel,
        out_shape=(
            jax.ShapeDtypeStruct(values.shape, BF16),
            jax.ShapeDtypeStruct((pairs, 1, 128), I32),
        ),
        in_specs=[SMEM, VMEM, VMEM],
        out_specs=(VMEM, VMEM),
        compiler_params=params(),
        name="order_blocks",
    )(ids, values, labels)


def exchange_kernel(x_ref, m_ref, ox_ref, om_ref, sx, rx, sm, rm, lsem):
    n = x_ref.shape[0]
    me = lax.axis_index("docs")
    barrier = pltpu.get_barrier_semaphore()

    def greet(i, carry):
        peer = lax.rem(me + i, n)
        pl.semaphore_signal(barrier, inc=1, device_id={"docs": peer}, device_id_type=MESH)
        return carry

    lax.fori_loop(1, n, greet, 0)
    own_x = pltpu.make_async_copy(x_ref.at[me], ox_ref.at[me], lsem.at[0])
    own_m = pltpu.make_async_copy(m_ref.at[me], om_ref.at[me], lsem.at[1])
    own_x.start()
    own_m.start()
    pl.semaphore_wait(barrier, n - 1)

    def copies(peer, slot):
        one = pltpu.make_async_remote_copy(
            src_ref=x_ref.at[peer], dst_ref=ox_ref.at[slot],
            send_sem=sx.at[peer], recv_sem=rx.at[slot],
            device_id={"docs": peer}, device_id_type=MESH,
        )
        two = pltpu.make_async_remote_copy(
            src_ref=m_ref.at[peer], dst_ref=om_ref.at[slot],
            send_sem=sm.at[peer], recv_sem=rm.at[slot],
            device_id={"docs": peer}, device_id_type=MESH,
        )
        return one, two

    def send(i, carry):
        one, two = copies(lax.rem(me + i, n), me)
        two.start()
        one.start()
        return carry

    lax.fori_loop(1, n, send, 0)
    own_x.wait()
    own_m.wait()

    def finish(i, carry):
        peer = lax.rem(me + i, n)
        one, two = copies(peer, peer)
        one.wait_recv()
        two.wait_recv()
        one.wait_send()
        two.wait_send()
        return carry

    lax.fori_loop(1, n, finish, 0)


def exchange(x, m):
    n = x.shape[0]
    return pl.pallas_call(
        exchange_kernel,
        out_shape=(jax.ShapeDtypeStruct(x.shape, x.dtype), jax.ShapeDtypeStruct(m.shape, m.dtype)),
        in_specs=[VMEM, VMEM],
        out_specs=(VMEM, VMEM),
        scratch_shapes=[DMA((n,)), DMA((n,)), DMA((n,)), DMA((n,)), DMA((2,))],
        compiler_params=params(0),
        name="exchange_blocks",
    )(x, m)


def sums_kernel(tiles, code_ref, x_ref, m_ref, sums_ref, sq_ref):
    n, rows, _ = x_ref.shape
    sums_ref[...] = jnp.zeros_like(sums_ref)
    cluster = lax.broadcasted_iota(I32, (K, rows), 0)

    def step(i, carry):
        spots, sums = [], []
        for u in range(4):
            a = 4 * i + u
            hot = jnp.where(cluster == m_ref[a][:, :rows], 1.0, 0.0).astype(BF16)
            sums.append(jnp.dot(hot, x_ref[a], preferred_element_type=F32))
            spots.append(code_ref[a, 0, rows] // tiles)
        for spot, part in zip(spots, sums):
            sums_ref[spot] += part
        return carry

    lax.fori_loop(0, n // 4, step, 0)

    def square(c, total):
        s = sums_ref[c]
        return total + s * s

    total = lax.fori_loop(0, sums_ref.shape[0], square, jnp.zeros((K, 128), F32))
    sq_ref[...] = dot_t(jnp.ones((8, 128), F32), total, HI)[:1]


def own_sums(tiles, code, x, m):
    return pl.pallas_call(
        functools.partial(sums_kernel, tiles),
        out_shape=(
            jax.ShapeDtypeStruct((BLK_OWN, K, 128), F32),
            jax.ShapeDtypeStruct((1, K), F32),
        ),
        in_specs=[SMEM, VMEM, VMEM],
        out_specs=(VMEM, VMEM),
        compiler_params=params(),
        cost_estimate=cost(17),
        name="own_sums",
    )(code, x, m)


def norm_kernel(ny, sq_ref, scale_ref, slots, zslots, stage, ssem, rsem, zssem, zrsem):
    x, z, core, y = coords()
    group = NX * ny * NC
    me = (x * ny + y) * NC + core
    barrier = pltpu.get_barrier_semaphore()

    def member(g):
        return dev(g // (ny * NC), z, lax.rem(g, NC), lax.rem(g // NC, ny))

    def greet(i, carry):
        pl.semaphore_signal(
            barrier, inc=1, device_id=member(lax.rem(me + i, group)), device_id_type=MESH
        )
        return carry

    lax.fori_loop(1, group, greet, 0)
    for i in range(1, NZ):
        pl.semaphore_signal(
            barrier, inc=1, device_id=dev(x, lax.rem(z + i, NZ), core, y), device_id_type=MESH
        )
    slots[me] = sq_ref[...]
    pl.semaphore_wait(barrier, group - 1 + NZ - 1)

    def copy(peer, slot):
        return pltpu.make_async_remote_copy(
            src_ref=sq_ref, dst_ref=slots.at[slot],
            send_sem=ssem.at[peer], recv_sem=rsem.at[slot],
            device_id=member(peer), device_id_type=MESH,
        )

    def send(i, carry):
        copy(lax.rem(me + i, group), me).start()
        return carry

    lax.fori_loop(1, group, send, 0)

    def finish(i, carry):
        peer = lax.rem(me + i, group)
        done = copy(peer, peer)
        done.wait_recv()
        done.wait_send()
        return carry

    lax.fori_loop(1, group, finish, 0)
    total = jnp.sum(slots[...], axis=0)
    stage[...] = total
    zslots[z] = total

    def zcopy(peer, slot):
        return pltpu.make_async_remote_copy(
            src_ref=stage, dst_ref=zslots.at[slot],
            send_sem=zssem.at[peer], recv_sem=zrsem.at[slot],
            device_id=dev(x, peer, core, y), device_id_type=MESH,
        )

    for i in range(1, NZ):
        zcopy(lax.rem(z + i, NZ), z).start()
    for i in range(1, NZ):
        peer = lax.rem(z + i, NZ)
        done = zcopy(peer, peer)
        done.wait_recv()
        done.wait_send()
    scale_ref[...] = lax.rsqrt(jnp.sum(zslots[...], axis=0) + EPSILON)


def norm_scale(ny, sq):
    group = NX * ny * NC
    return pl.pallas_call(
        functools.partial(norm_kernel, ny),
        out_shape=jax.ShapeDtypeStruct((1, K), F32),
        in_specs=[VMEM],
        out_specs=VMEM,
        scratch_shapes=[
            pltpu.VMEM((group, 1, K), F32),
            pltpu.VMEM((NZ, 1, K), F32),
            pltpu.VMEM((1, K), F32),
            DMA((group,)), DMA((group,)), DMA((NZ,)), DMA((NZ,)),
        ],
        compiler_params=params(1),
        cost_estimate=cost(17),
        name="norm_scale",
    )(sq)


def axis_peers(ny):
    x, z, core, y = coords()
    peers = {
        "c": [dev(x, z, lax.rem(core + i, NC), y) for i in range(1, NC)],
        "x": [dev(lax.rem(x + i, NX), z, core, y) for i in range(1, NX)],
        "z": [dev(x, lax.rem(z + i, NZ), core, y) for i in range(1, NZ)],
        "y": [dev(x, z, core, lax.rem(y + i, ny)) for i in range(1, ny)],
    }
    return (x, z, core, y), peers


def greet_axes(peers):
    barrier = pltpu.get_barrier_semaphore()
    count = 0
    for axis in "cyxz":
        for peer in peers[axis]:
            pl.semaphore_signal(barrier, inc=1, device_id=peer, device_id_type=MESH)
            count += 1
    return barrier, count


def spread(pos, size, peers, source, target, ssem, rsem):
    def copy(i, send):
        p = lax.rem(pos + i, size)
        return pltpu.make_async_remote_copy(
            src_ref=source(p), dst_ref=target(pos if send else p),
            send_sem=ssem.at[p], recv_sem=rsem.at[pos if send else p],
            device_id=peers[i - 1], device_id_type=MESH,
        )

    for i in range(1, size):
        copy(i, True).start()

    def finish():
        for i in range(1, size):
            done = copy(i, False)
            done.wait_recv()
            done.wait_send()

    return finish


def block_inverse(d):
    n = d.shape[0]
    eye = (lax.broadcasted_iota(I32, (n, n), 0) == lax.broadcasted_iota(I32, (n, n), 1)).astype(F32)
    trace = jnp.sum(d * eye)
    widest = jnp.max(jnp.sum(jnp.abs(d), axis=1, keepdims=True))
    bound = jnp.minimum(trace, widest)
    low = 1.0 / bound
    inv = eye * (1.0 / bound)
    for _ in range(NEWTON_STEPS):
        inv = inv * (2.0 / (1.0 + low))
        left = jnp.dot(d, inv, precision=HI, preferred_element_type=F32)
        inv = 2.0 * inv - jnp.dot(inv, left, precision=HI, preferred_element_type=F32)
        low = 4.0 * low / ((1.0 + low) * (1.0 + low))
    return inv


def scores_kernel(tiles, parts, width, *refs):
    first_ref, scale_ref = refs[0], refs[1]
    groups = [refs[2 + 3 * g: 5 + 3 * g] for g in range(len(parts))]
    out_ref, sums_ref, con_ref = refs[2 + 3 * len(parts):]
    rows = groups[0][1].shape[1]
    sums_ref[...] = jnp.zeros_like(sums_ref)
    out_ref[...] = jnp.zeros_like(out_ref)
    cluster = lax.broadcasted_iota(I32, (width, rows), 0) + first_ref[0]

    for (start, count, base), (code_ref, x_ref, m_ref) in zip(parts, groups):
        def add(i, carry):
            spots, sums = [], []
            for u in range(UNROLL):
                a = start + UNROLL * i + u
                hot = jnp.where(cluster == m_ref[a][:, :rows], 1.0, 0.0).astype(BF16)
                sums.append(jnp.dot(hot, x_ref[UNROLL * i + u], preferred_element_type=F32))
                spots.append(code_ref[a, 0, rows] // tiles + base)
            for spot, part in zip(spots, sums):
                sums_ref[spot] += part
            return carry

        lax.fori_loop(0, count // UNROLL, add, 0)

    mine = scale_ref[:, pl.ds(pl.multiple_of(first_ref[0], width), width)]
    scale = jnp.broadcast_to(mine, (128, width)).T

    def normalise(b, carry):
        con_ref[b] = (sums_ref[b] * scale).astype(BF16)
        return carry

    lax.fori_loop(0, sums_ref.shape[0], normalise, 0)

    for (start, count, base), (code_ref, x_ref, m_ref) in zip(parts, groups):
        def score(i, carry):
            spots, values = [], []
            for u in range(UNROLL):
                a = start + UNROLL * i + u
                code = code_ref[a, 0, rows]
                values.append(dot_t(x_ref[UNROLL * i + u], con_ref[code // tiles + base]))
                spots.append((a, lax.rem(code, tiles)))
            for (a, tile), value in zip(spots, values):
                out_ref[a, tile] += value
            return carry

        lax.fori_loop(0, count // UNROLL, score, 0)


def partial_scores(tiles, width, first, scale, parts, arrays):
    n = arrays[0][2].shape[0]
    rows = arrays[0][1].shape[1]
    ny = K // width
    flat = [a for group in arrays for a in group]
    return pl.pallas_call(
        functools.partial(scores_kernel, tiles, parts, width),
        out_shape=jax.ShapeDtypeStruct((n, tiles, rows, width), F32),
        in_specs=[SMEM, VMEM] + [SMEM, VMEM, VMEM] * len(parts),
        out_specs=VMEM,
        scratch_shapes=[
            pltpu.VMEM((ny * BLK_OWN, width, 128), F32),
            pltpu.VMEM((ny * BLK_OWN, width, 128), BF16),
        ],
        compiler_params=params(),
        cost_estimate=cost(45),
        name="partial_scores",
    )(first, scale, *flat)


def gram_part(sums_ref, scale_ref, part):
    scale = jnp.broadcast_to(scale_ref[...], (128, K)).T
    part[...] = jnp.zeros_like(part)
    chunk = 4

    def step(i, carry):
        pieces = [(sums_ref[i * chunk + j] * scale).astype(BF16) for j in range(chunk)]
        c = jnp.concatenate(pieces, axis=1)
        part[...] += dot_t(c, c).reshape(part.shape)
        return carry

    lax.fori_loop(0, sums_ref.shape[0] // chunk, step, 0)


def inverse_panel(a_ref, p):
    n = 128
    cut = slice(p * n, (p + 1) * n)
    inv = block_inverse(a_ref[cut, cut])
    row = jnp.dot(inv, a_ref[cut, :], precision=HI, preferred_element_type=F32)
    col = a_ref[:, cut]
    for q in range(K // n):
        if q == p:
            continue
        rest = slice(q * n, (q + 1) * n)
        c = col[rest]
        a_ref[rest, :] -= jnp.dot(c, row, precision=HI, preferred_element_type=F32)
        a_ref[rest, cut] = -jnp.dot(c, inv, precision=HI, preferred_element_type=F32)
    a_ref[cut, :] = row
    a_ref[cut, cut] = inv


def reduce_kernel(ny, s_ref, sums_hbm, scale_ref, scores_ref, a_ref,
                  rc, acc, rx, rn, rf, lsem, sums_ref,
                  part, gc, a1, gy, a2, gx, a3, gz, gram,
                  cs, cr, xs, xr, zs, zr, ys, yr,
                  gcs, gcr, gys, gyr, gxs, gxr, gzs, gzr,
                  gxs2, gxr2, gys2, gyr2, gcs2, gcr2):
    (x, z, core, y), peers = axis_peers(ny)
    barrier, count = greet_axes(peers)
    width = rc.shape[-1]
    order = [lax.rem(x + i, NX) for i in (NX - 1, 1, 2, 0)]
    load = pltpu.make_async_copy(sums_hbm, sums_ref, lsem.at[NX])
    load.start()
    own = []
    for i, p in enumerate(order):
        copy = pltpu.make_async_copy(s_ref.at[p, :, core], acc.at[p], lsem.at[i])
        copy.start()
        own.append(copy)
    pl.semaphore_wait(barrier, count)
    swap = []
    for i, p in enumerate(order):
        copy = pltpu.make_async_remote_copy(
            src_ref=s_ref.at[p, :, NC - 1 - core], dst_ref=rc.at[p],
            send_sem=cs.at[i], recv_sem=cr.at[i],
            device_id=peers["c"][0], device_id_type=MESH,
        )
        copy.start()
        swap.append(copy)

    def pair(i):
        own[i].wait()
        swap[i].wait_recv()
        acc[order[i]] += rc[order[i]]

    cut = NZ // 2
    upper, lower = peers["x"][0], peers["x"][NX - 2]

    def hop(s, down, sub):
        sent = lax.rem(x + (s + 1 if down else 2 * NX - s - 1), NX)
        part_z = pl.ds(down * cut + sub * (cut // 2), cut // 2)
        sem = 4 * s + 2 * down + sub
        return pltpu.make_async_remote_copy(
            src_ref=acc.at[sent, part_z], dst_ref=rx.at[s, part_z],
            send_sem=xs.at[sem], recv_sem=xr.at[sem],
            device_id=lower if down else upper, device_id_type=MESH,
        )

    def land(s, sub):
        for down in range(2):
            hop(s, down, sub).wait_recv()
            got = lax.rem(x + (s + 2 if down else 2 * NX - s - 2), NX)
            part_z = pl.ds(down * cut + sub * (cut // 2), cut // 2)
            acc[got, part_z] += rx[s, part_z]

    def go(s, sub):
        for down in range(2):
            hop(s, down, sub).start()

    docs = rc.shape[2]

    def ahead(side, reach):
        return lax.rem(z + (NZ - reach if side else reach), NZ)

    def part_d(side):
        return pl.ds(side * (docs // 2), docs // 2)

    def zcopy(source, target, sem, p):
        return pltpu.make_async_remote_copy(
            src_ref=source, dst_ref=target, send_sem=zs.at[sem], recv_sem=zr.at[sem],
            device_id=dev(x, p, core, y), device_id_type=MESH,
        )

    def far(side):
        return zcopy(acc.at[x, ahead(side, 3)], rf.at[side], side, ahead(side, 1))

    def fourth(side):
        return zcopy(acc.at[x, ahead(side, 4), part_d(side)], rf.at[2, part_d(side)],
                     2 + side, ahead(side, 2))

    def near(side, reach):
        slot = 2 * reach - 2 + side
        return zcopy(acc.at[x, ahead(side, reach)], rn.at[slot], 4 + slot, ahead(side, reach))

    blocks = part.shape[0]
    half = blocks // NC
    quarter = half // ny

    load.wait()
    gram_part(sums_ref, scale_ref, part)
    finish = spread(core, NC, peers["c"],
                    lambda p: part.at[pl.ds(p * half, half)], lambda p: gc, gcs, gcr)
    pair(0)
    for sub in range(2):
        hop(0, 0, sub).start()
    pair(1)
    for sub in range(2):
        hop(0, 1, sub).start()
    finish()
    a1[...] = part[pl.ds(core * half, half)] + gc[...]
    finish = spread(y, ny, peers["y"],
                    lambda p: a1.at[pl.ds(p * quarter, quarter)], lambda p: gy.at[p], gys, gyr)
    pair(2)
    pair(3)
    gy[y] = a1[pl.ds(y * quarter, quarter)]
    finish()
    total = gy[0]
    for i in range(1, ny):
        total = total + gy[i]
    a2[...] = total
    finish = spread(x, NX, peers["x"], lambda p: a2.at[p], lambda p: gx.at[p], gxs, gxr)
    gx[x] = a2[x]
    land(0, 0)
    go(1, 0)
    finish()
    total = gx[0]
    for i in range(1, NX):
        total = total + gx[i]
    a3[...] = total
    gz[z] = total
    finish = spread(z, NZ, peers["z"], lambda p: a3, lambda p: gz.at[p], gzs, gzr)
    land(0, 1)
    finish()
    total = gz[0]
    for i in range(1, NZ):
        total = total + gz[i]
    base = core * half + y * quarter
    gram[base + x] = total
    finish = spread(x, NX, peers["x"], lambda p: gram.at[base + x],
                    lambda p: gram.at[base + p], gxs2, gxr2)
    go(1, 1)
    land(1, 0)
    go(2, 0)
    finish()
    finish = spread(y, ny, peers["y"], lambda p: gram.at[pl.ds(base, quarter)],
                    lambda p: gram.at[pl.ds(core * half + p * quarter, quarter)], gys2, gyr2)
    land(1, 1)
    go(2, 1)
    finish()
    spread(core, NC, peers["c"], lambda p: gram.at[pl.ds(core * half, half)],
           lambda p: gram.at[pl.ds(p * half, half)], gcs2, gcr2)()

    eye = (lax.broadcasted_iota(I32, (K, K), 0) == lax.broadcasted_iota(I32, (K, K), 1)).astype(F32)
    a_ref[...] = gram[...].reshape(K, K) + RIDGE_WEIGHT * eye
    land(2, 0)
    land(2, 1)
    for side in range(2):
        far(side).start()
        fourth(side).start()
    for side in range(2):
        near(side, 1).start()
    inverse_panel(a_ref, 0)
    for side in range(2):
        far(side).wait_recv()
        fourth(side).wait_recv()
        p = ahead(side, 2)
        acc[x, p] += rf[side]
        acc[x, p, part_d(side)] += rf[2, part_d(side)]
        near(side, 2).start()
    inverse_panel(a_ref, 1)
    inverse_panel(a_ref, 2)
    total = acc[x, z]
    for side in range(2):
        for reach in range(1, 3):
            near(side, reach).wait_recv()
            total = total + rn[2 * reach - 2 + side]

    def lanes(p):
        return pl.ds(pl.multiple_of(p * width, width), width)

    scores_ref[:, lanes(y)] = total
    finish = spread(y, ny, peers["y"], lambda p: scores_ref.at[:, lanes(y)],
                    lambda p: scores_ref.at[:, lanes(p)], ys, yr)
    inverse_panel(a_ref, 3)
    finish()
    for side in range(2):
        for copy in (far(side), fourth(side), near(side, 1), near(side, 2)):
            copy.wait_send()
    for copy in swap:
        copy.wait_send()
    for s in range(NX - 1):
        for down in range(2):
            for sub in range(2):
                hop(s, down, sub).wait_send()


def reduce_scores(ny, partial, sums, scale):
    n, tiles, rows, width = partial.shape
    docs = tiles * rows
    part_rows = K // (NC * ny * NX)
    blocks = K // part_rows
    half, quarter = blocks // NC, blocks // (NC * ny)
    sems = []
    for size in (NX, 4 * (NX - 1), NZ, ny, NC, ny, NX, NZ, NX, ny, NC):
        sems += [DMA((size,)), DMA((size,))]
    return pl.pallas_call(
        functools.partial(reduce_kernel, ny),
        out_shape=(jax.ShapeDtypeStruct((docs, K), F32), jax.ShapeDtypeStruct((K, K), F32)),
        in_specs=[ANY, ANY, VMEM],
        out_specs=(VMEM, VMEM),
        scratch_shapes=[
            pltpu.VMEM((NX, NZ, docs, width), F32),
            pltpu.VMEM((NX, NZ, docs, width), F32),
            pltpu.VMEM((NX - 1, NZ, docs, width), F32),
            pltpu.VMEM((4, docs, width), F32),
            pltpu.VMEM((3, docs, width), F32),
            DMA((NX + 1,)),
            pltpu.VMEM(sums.shape, F32),
            pltpu.VMEM((blocks, part_rows, K), F32),
            pltpu.VMEM((half, part_rows, K), F32),
            pltpu.VMEM((half, part_rows, K), F32),
            pltpu.VMEM((ny, quarter, part_rows, K), F32),
            pltpu.VMEM((quarter, part_rows, K), F32),
            pltpu.VMEM((NX, part_rows, K), F32),
            pltpu.VMEM((part_rows, K), F32),
            pltpu.VMEM((NZ, part_rows, K), F32),
            pltpu.VMEM((blocks, part_rows, K), F32),
        ] + sems,
        compiler_params=params(2),
        name="reduce_scores",
    )(partial.reshape(NX, NZ, NC, docs, width), sums, scale)


def shift(array, ny, by):
    return lax.ppermute(array, "terms", [(i, (i + by) % ny) for i in range(ny)])


def body(values, block_ids, assignment):
    tiles, slots, rows, block_width = values.shape
    ny = lax.axis_size("terms")
    pairs = tiles * slots
    width = K // ny
    y = lax.axis_index("terms")
    labels = jnp.pad(
        assignment.reshape(tiles, 1, rows), ((0, 0), (0, 0), (0, 128 - rows)), constant_values=-1
    )
    ordered, meta = order_blocks(
        values.reshape(pairs, rows, block_width), block_ids, labels
    )
    own_x, own_m = exchange(ordered, meta)

    half = pairs // 2
    arrays, parts = [(own_m, own_x, own_m)], [(0, pairs, 0)]
    up_x, down_x = shift(own_x, ny, 1), shift(own_x, ny, -1)
    up_m = shift(own_m, ny, 1)
    arrays.append((up_m, up_x, up_m))
    parts.append((0, pairs, BLK_OWN))
    if ny > 2:
        down_m, far_m = shift(own_m, ny, -1), shift(own_m, ny, 2)
        far_a = shift(up_x[:half], ny, 1)
        far_b = shift(down_x[half:], ny, -1)
        arrays.append((down_m, down_x, down_m))
        parts.append((0, pairs, 3 * BLK_OWN))
        arrays.append((far_m, far_a, far_m))
        parts.append((0, half, 2 * BLK_OWN))
        arrays.append((far_m, far_b, far_m))
        parts.append((half, half, 2 * BLK_OWN))

    sums, sq = own_sums(tiles, own_m, own_x, own_m)
    scale = norm_scale(ny, sq)
    first = (y * width).reshape(1)
    partial = partial_scores(tiles, width, first, scale, tuple(parts), arrays)
    scores, inverse = reduce_scores(ny, partial, sums, scale)
    inverse_cols = lax.dynamic_slice_in_dim(inverse, y * width, width, 1)
    return jnp.dot(scores, inverse_cols, precision=HI, preferred_element_type=F32)


def solution(mesh):
    in_specs = (P("docs", "terms", None, None), P("docs", "terms"), P("docs", None))
    out_specs = P("docs", "terms")
    return jax.shard_map(body, mesh=mesh, in_specs=in_specs, out_specs=out_specs, check_vma=False)
```
